32 devices in a mesh: groups: 2 (over y), ctx: 4 (over x, core), mp: 4 (over z).
Axes of the slice: x: 2, y: 2, z: 4, core: 2. Of those that a mesh axis runs over, the one named last changes fastest.
Arguments:
- tokens: bfloat16 [3072, 8192], P(('groups', 'ctx')), parts along dimension 0, may hold values from -6 to 6
- norm_gain: bfloat16 [8192], replicated, may hold values from 0.099609375 to 1.8984375
- w_query: bfloat16 [8192, 4096], P('ctx', 'mp'), may hold values from -0.44194174 to 0.44194174
- w_key: bfloat16 [8192, 1024], P('ctx', 'mp'), may hold values from -0.044194174 to 0.044194174
- value_weight: bfloat16 [8192, 1024], P('ctx', 'mp'), may hold values from -0.0625 to 0.0625
- slab_order: int32 [8], P('groups'), parts along dimension 0, may hold values from 0 to 3, each once
- segment_ids: int32 [3072], P('groups'), parts along dimension 0, may hold values from 0 to 3, as said below
Outputs:
- attended: bfloat16 [3072, 4096], P(('groups', 'ctx'), 'mp'), parts along dimension 0
The draws below stay inside these ranges and needn't reach their ends.
There are 2 independent parts, one for each index of `groups`. The reference program is written for one: setup_inputs(seed, part) draws one part's arguments, and reference() takes and returns one part's arrays. A program takes and returns all parts, laid end to end along the dimension named above; an argument that names none is the same for every part. Nothing has to cross between parts.
Inputs may be any that keep to these rules, and one draw needn't show every extreme that they name: `segment_ids`: never falling along positions; each of the 4 segments holds at least one position.
All inputs are finite; a program needn't handle non-finite values.
Results may differ from the reference program's by a relative error of at most 0.012.
Values may be sent and summed in bfloat16 or wider, within the bound.
A program may use at most 128 MiB of HBM per device.

```python
import math
import jax
import jax.numpy as jnp
from jax import lax

MODEL_WIDTH = 8192
QUERY_HEADS = 32
KEY_VALUE_HEADS = 8
HEAD_SIZE = 128
SLABS = 4
TOKENS = 1536


def attention_pair(key):
    base = jax.random.fold_in(key, 11)
    leading_key = jax.random.fold_in(base, 1)
    second_key = jax.random.fold_in(base, 2)
    key_matrix = jnp.clip(jax.random.normal(leading_key, (MODEL_WIDTH, KEY_VALUE_HEADS * HEAD_SIZE), jnp.float32), -4.0, 4.0) * MODEL_WIDTH ** (-0.5)
    noise = jnp.clip(jax.random.normal(second_key, (MODEL_WIDTH, QUERY_HEADS * HEAD_SIZE), jnp.float32), -4.0, 4.0) * (3.0 * MODEL_WIDTH ** (-0.5))
    query_weight = noise
    return (query_weight, key_matrix)


def draw_w_query(key, part):
    query_weight, key_matrix = attention_pair(key)
    return query_weight.astype(jnp.bfloat16)


def draw_w_key(key, part):
    query_weight, key_matrix = attention_pair(key)
    return key_matrix.astype(jnp.bfloat16)


def draw_segment_ids(key, part):
    cut_key = jax.random.fold_in(key, 5)
    cuts = jax.random.permutation(cut_key, jnp.arange(TOKENS - 1, dtype=jnp.int32))[:3] + 1
    places = jnp.arange(TOKENS, dtype=jnp.int32)
    return jnp.sum((places[:, None] >= cuts[None, :]).astype(jnp.int32), axis=1).astype(jnp.int32)


def block_levels(rng, dims, pieces, smallest, largest):
    loudness = 1.0
    for dim, parts in pieces:
        draws = jax.random.uniform(jax.random.fold_in(jax.random.fold_in(rng, 6), dim), (parts,), jnp.float32, smallest / len(pieces), largest / len(pieces))
        loudness = loudness * jnp.repeat(jnp.exp(draws), dims[dim] // parts).reshape((-1,) + (1,) * (len(dims) - 1 - dim))
    return loudness


def normal_values(own_key, dims, deviation, limit, pieces=(), held_as=jnp.bfloat16):
    loudness = block_levels(own_key, dims, pieces, -0.22, 0.18) if pieces else 1.0
    array = jax.random.normal(own_key, dims, jnp.float32) * deviation * loudness
    return jnp.minimum(jnp.maximum(array, -limit), limit).astype(held_as)


def setup_inputs(seed: int = 0, part: int = 0) -> dict:
    arg_keys = jax.random.split(jax.random.key(seed), 8)
    part_keys = jax.random.split(jax.random.fold_in(arg_keys[7], part), 8)
    return {
        "tokens": normal_values(part_keys[0], (TOKENS, MODEL_WIDTH), 1.0, 6.0, ((0, 4),)),
        "norm_gain": jnp.clip(1.0 + 0.18 * jax.random.normal(arg_keys[1], (MODEL_WIDTH,), jnp.float32), 0.099609375, 1.8984375).astype(jnp.bfloat16),
        "w_query": draw_w_query(jax.random.fold_in(arg_keys[7], 71), part),
        "w_key": draw_w_key(jax.random.fold_in(arg_keys[7], 71), part),
        "value_weight": normal_values(arg_keys[4], (MODEL_WIDTH, KEY_VALUE_HEADS * HEAD_SIZE), MODEL_WIDTH ** -0.5, 0.0625, ((0, 4), (1, 4))),
        "slab_order": jax.random.permutation(part_keys[5], SLABS).astype(jnp.int32),
        "segment_ids": draw_segment_ids(jax.random.fold_in(jax.random.fold_in(arg_keys[7], part), 71), part),
    }


def apply_rotary(values, positions, heads):
    width = values.shape[1] // heads
    half = width // 2
    freqs = jnp.exp(jnp.arange(half, dtype=jnp.float32) * (-2.0 * math.log(500000.0) / width))
    angles = positions.astype(jnp.float32)[:, None] * freqs[None, :]
    cosine = jnp.cos(angles)[:, None, :]
    sine = jnp.sin(angles)[:, None, :]
    shaped = values.reshape(values.shape[0], heads, width)
    first = shaped[..., :half]
    second = shaped[..., half:]
    turned = jnp.concatenate([first * cosine - second * sine, second * cosine + first * sine], axis=-1)
    return turned.reshape(values.shape)

def reference(tokens, norm_gain, w_query, w_key, value_weight, slab_order, segment_ids):
    seq_len = tokens.shape[0]
    slab_rows = seq_len // SLABS
    token_position = (slab_order[:, None] * slab_rows + jnp.arange(slab_rows, dtype=jnp.int32)[None, :]).reshape(-1).astype(jnp.int32)
    segment = jnp.take(segment_ids, token_position)
    floats = tokens.astype(jnp.float32)
    inverse = lax.rsqrt(lax.optimization_barrier(jnp.mean(floats * floats, axis=-1, keepdims=True)) + 1e-05)
    normed = (floats * inverse * norm_gain.astype(jnp.float32)[None, :]).astype(jnp.bfloat16)
    query = jnp.dot(normed, w_query, preferred_element_type=jnp.float32)
    key_projected = jnp.dot(normed, w_key, preferred_element_type=jnp.float32)
    value_proj = jnp.dot(normed, value_weight, preferred_element_type=jnp.float32)
    query_rot = apply_rotary(query, token_position, QUERY_HEADS).astype(jnp.bfloat16)
    key_rotary = apply_rotary(key_projected, token_position, KEY_VALUE_HEADS).astype(jnp.bfloat16)
    value_b = value_proj.astype(jnp.bfloat16)
    group_width = QUERY_HEADS // KEY_VALUE_HEADS
    allowed = (token_position[None, :] <= token_position[:, None]) & (segment[None, :] == segment[:, None])
    scale = HEAD_SIZE ** (-0.5)

    def one_head(head):
        kv_head = head // group_width
        query_head = lax.dynamic_slice_in_dim(query_rot, head * HEAD_SIZE, HEAD_SIZE, 1)
        key_head = lax.dynamic_slice_in_dim(key_rotary, kv_head * HEAD_SIZE, HEAD_SIZE, 1)
        value_head = lax.dynamic_slice_in_dim(value_b, kv_head * HEAD_SIZE, HEAD_SIZE, 1)
        scores = jnp.dot(query_head, key_head.T, preferred_element_type=jnp.float32) * scale
        scores = jnp.where(allowed, scores, -1e+30)
        row_peak = lax.optimization_barrier(jnp.max(scores, axis=-1, keepdims=True))
        exps = jnp.where(allowed, jnp.exp(scores - row_peak), 0.0)
        weights = exps.astype(jnp.bfloat16)
        mixed = jnp.dot(weights, value_head, preferred_element_type=jnp.float32)
        return (mixed / lax.optimization_barrier(jnp.sum(exps, axis=-1, keepdims=True))).astype(jnp.bfloat16)
    per_head = lax.map(one_head, jnp.arange(QUERY_HEADS, dtype=jnp.int32))
    return jnp.transpose(per_head, (1, 0, 2)).reshape(seq_len, QUERY_HEADS * HEAD_SIZE)
```

```python
import math

import jax
import jax.numpy as jnp
from jax import lax
from jax.experimental import pallas as pl
from jax.experimental.pallas import tpu as pltpu
from jax.sharding import PartitionSpec as P

HEAD_SIZE = 128


def apply_rotary(values, positions, heads):
    width = values.shape[1] // heads
    half = width // 2
    freqs = jnp.exp(jnp.arange(half, dtype=jnp.float32) * (-2.0 * math.log(500000.0) / width))
    angles = positions.astype(jnp.float32)[:, None] * freqs[None, :]
    cosine = jnp.cos(angles)[:, None, :]
    sine = jnp.sin(angles)[:, None, :]
    shaped = values.reshape(values.shape[0], heads, width)
    first = shaped[..., :half]
    second = shaped[..., half:]
    turned = jnp.concatenate(
        [first * cosine - second * sine, second * cosine + first * sine], axis=-1
    )
    return turned.reshape(values.shape)


def local_plain(tokens, norm_gain, w_query, w_key, value_weight, slab_order, segment_ids):
    tok_rows = tokens.shape[0]
    device_slab = lax.axis_index("ctx")
    position_all = (
        slab_order[:, None] * tok_rows + jnp.arange(tok_rows, dtype=jnp.int32)[None, :]
    ).reshape(-1)
    segment_all = jnp.take(segment_ids, position_all)
    my_position = lax.dynamic_slice_in_dim(position_all, device_slab * tok_rows, tok_rows)
    my_segment = lax.dynamic_slice_in_dim(segment_all, device_slab * tok_rows, tok_rows)
    floats = tokens.astype(jnp.float32)
    inverse = lax.rsqrt(jnp.mean(floats * floats, axis=-1, keepdims=True) + 1e-05)
    normed = (floats * inverse * norm_gain.astype(jnp.float32)[None, :]).astype(jnp.bfloat16)
    query_cols = w_query.shape[1]
    key_cols = w_key.shape[1]
    query = jnp.dot(
        normed,
        lax.all_gather(w_query, "ctx", axis=0, tiled=True),
        preferred_element_type=jnp.float32,
    )
    key_projected = jnp.dot(
        normed, lax.all_gather(w_key, "ctx", axis=0, tiled=True), preferred_element_type=jnp.float32
    )
    value_proj = jnp.dot(
        normed,
        lax.all_gather(value_weight, "ctx", axis=0, tiled=True),
        preferred_element_type=jnp.float32,
    )
    head_size = HEAD_SIZE
    heads_here = query_cols // head_size
    kv_here = key_cols // head_size
    group_width = heads_here // kv_here
    query_rot = (
        apply_rotary(query, my_position, heads_here)
        .astype(jnp.bfloat16)
        .reshape(tok_rows, kv_here, group_width, head_size)
    )
    key_rotary = apply_rotary(key_projected, my_position, kv_here).astype(jnp.bfloat16)
    value_b = value_proj.astype(jnp.bfloat16)
    scale = head_size ** (-0.5)
    start_state = (
        jnp.full((kv_here, group_width, tok_rows), -1e30, jnp.float32),
        jnp.zeros((kv_here, group_width, tok_rows), jnp.float32),
        jnp.zeros((kv_here, group_width, tok_rows, head_size), jnp.float32),
    )
    state = start_state
    key_piece = lax.all_gather(key_rotary, "ctx", axis=0, tiled=True)
    value_piece = lax.all_gather(value_b, "ctx", axis=0, tiled=True)
    piece_rows = key_piece.shape[0]
    block_rows = math.gcd(piece_rows, 1024)
    block_count = piece_rows // block_rows
    key_blocks = key_piece.reshape(block_count, block_rows, kv_here, head_size)
    value_blocks = value_piece.reshape(block_count, block_rows, kv_here, head_size)
    key_positions = position_all.reshape(block_count, block_rows)
    key_segments = segment_all.reshape(block_count, block_rows)

    def advance(inner, item):
        key_block, value_block, block_positions, block_segments = item
        allowed = (block_positions[None, :] <= my_position[:, None]) & (
            block_segments[None, :] == my_segment[:, None]
        )
        running_max, running_sum, running_acc = inner
        scores = (
            jnp.einsum("tkgd,nkd->kgtn", query_rot, key_block, preferred_element_type=jnp.float32)
            * scale
        )
        scores = jnp.where(allowed[None, None], scores, -1e30)
        new_max = jnp.maximum(running_max, jnp.max(scores, axis=-1))
        exps = jnp.where(allowed[None, None], jnp.exp(scores - new_max[..., None]), 0.0)
        factor = jnp.exp(running_max - new_max)
        new_sum = running_sum * factor + jnp.sum(exps, axis=-1)
        new_acc = running_acc * factor[..., None] + jnp.einsum(
            "kgtn,nkd->kgtd",
            exps.astype(jnp.bfloat16),
            value_block,
            preferred_element_type=jnp.float32,
        )
        inner = (new_max, new_sum, new_acc)
        return (inner, None)

    state, _ = lax.scan(advance, state, (key_blocks, value_blocks, key_positions, key_segments))
    final_max, final_sum, final_acc = state
    mixed = final_acc / final_sum[..., None]
    return (
        jnp.transpose(mixed, (2, 0, 1, 3))
        .reshape(tok_rows, heads_here * head_size)
        .astype(jnp.bfloat16)
    )


NEG = -1e30
PARTS = 6
SUBS = 4
LAG = 4


def fused_kernel(
    tokens, gain, w_query, w_key, w_value, slab_order, segments, out,
    wall, normed, gain_row, own, prem, xrem, skv, rkv, sq, rq, keep, qrot, kv, vt,
    table, places, lows, kbase, eye, peak, total, acc,
    tsem, wsem, ws, wr, xs, ins, outs, xr, kvs, kvr, qs, qr, cs, cr,
):
    g = lax.axis_index("groups")
    t = lax.axis_index("ctx")
    m = lax.axis_index("mp")
    x_index = t // 2
    core = t % 2
    t_core = x_index * 2 + (1 - core)
    t_x = (1 - x_index) * 2 + core
    middle = (m == 1) | (m == 2)
    core_dev = (g, t_core, m)
    x_dev = (g, t_x, m)
    inner_dev = (g, t, 1 + m % 2)
    outer_dev = (g, t, 3 * (m // 2))
    rows = tokens.shape[0]
    part = rows // PARTS
    depth = wall.shape[1]
    near = depth * SUBS
    kv_cols = w_key.shape[1]
    kv_heads = kv_cols // HEAD_SIZE
    both = 2 * kv_cols
    heads = w_query.shape[1] // HEAD_SIZE
    group_width = heads // kv_heads
    keys = 4 * part
    lanes = group_width * part

    def order(n):
        high = m // 2
        side = m + high * (3 - 2 * m)
        later = n // 3
        end = (2 * n) % 5 + 5 * (n // 5)
        mid = ((n % 3) * (1 + later) + 2 * (1 - later)) % 3 + 3 * later
        p = end * (1 - side) + mid * side
        return p + high * (5 - 2 * p)

    def part_rows(p):
        return pl.ds(pl.multiple_of(p * part, part), part)

    def remote(src, dst, send, recv, dev):
        return pltpu.make_async_remote_copy(
            src_ref=src, dst_ref=dst, send_sem=send, recv_sem=recv,
            device_id=dev, device_id_type=pl.DeviceIdType.MESH,
        )

    def sub(s):
        return (2 * core + s) % SUBS

    def token_load(p):
        return pltpu.make_async_copy(tokens.at[part_rows(p), :], normed.at[part_rows(p), :], tsem.at[p])

    sources = (
        (w_key, pl.ds(0, kv_cols)),
        (w_value, pl.ds(kv_cols, kv_cols)),
        (w_query, pl.ds(both, heads * HEAD_SIZE)),
    )

    def weight_load(i, j):
        source, columns = sources[j]
        return pltpu.make_async_copy(
            source.at[pl.ds(i * depth, depth), :], wall.at[2 * core + i, :, columns], wsem.at[i, j]
        )

    def weight_copy(i, j, c):
        source, columns = sources[j]
        return remote(
            source.at[pl.ds(i * depth, depth), :], wall.at[2 * c + i, :, columns],
            ws.at[i, j], wr.at[i, j], core_dev,
        )

    def token_send(n, p, k):
        columns = pl.ds(pl.multiple_of((1 - x_index) * near + k * depth, depth), depth)
        return remote(normed.at[part_rows(p), columns], xrem.at[p, k], xs.at[n // 2, k], xr.at[p, k], x_dev)

    def inner_send(n, p, k):
        return remote(xrem.at[p, k], xrem.at[p, k], ins.at[n, k], xr.at[p, k], inner_dev)

    def outer_send(n, p, k):
        return remote(xrem.at[p, k], xrem.at[p, k], outs.at[n, k], xr.at[p, k], outer_dev)

    def to_inner(n):
        return (n == 0) | (middle & (n <= 2))

    def to_outer(n):
        return middle & (n != 1) & (n != 5)

    def kv_send(n):
        return remote(skv.at[n], rkv.at[n], kvs.at[n], kvr.at[n], x_dev)

    def q_send(n):
        return remote(sq.at[n], rq.at[n], qs.at[n], qr.at[n], x_dev)

    def mate_copy(n, c):
        view = kv.at[n, pl.ds(pl.multiple_of(c * 2 * part, 2 * part), 2 * part), :]
        return remote(view, view, cs.at[n], cr.at[n], core_dev)

    for n in (0, 2, 1, 3, 4, 5):
        token_load(order(n)).start()
        if n == 0:
            for i in range(2):
                for j in range(3):
                    weight_load(i, j).start()

    barrier = pltpu.get_barrier_semaphore()
    for dev in (core_dev, x_dev, inner_dev):
        pl.semaphore_signal(barrier, inc=1, device_id=dev, device_id_type=pl.DeviceIdType.MESH)

    @pl.when(middle)
    def _():
        pl.semaphore_signal(barrier, inc=1, device_id=outer_dev, device_id_type=pl.DeviceIdType.MESH)

    gain_row[...] = gain[...].astype(jnp.float32).reshape(1, gain.shape[0])

    def norm_part(p):
        def norm_rows(i, carry):
            at = pl.ds(pl.multiple_of(p * part + i * 16, 16), 16)
            floats = normed[at, :].astype(jnp.float32)
            inverse = lax.rsqrt(jnp.mean(floats * floats, axis=-1, keepdims=True) + 1e-05)
            normed[at, :] = (floats * inverse * gain_row[...]).astype(jnp.bfloat16)
            return carry

        lax.fori_loop(0, part // 16, norm_rows, 0)

    token_load(order(0)).wait()
    norm_part(order(0))

    @pl.when(middle)
    def _():
        pl.semaphore_wait(barrier, 4)

    @pl.when(jnp.logical_not(middle))
    def _():
        pl.semaphore_wait(barrier, 3)

    for s in range(SUBS):
        token_send(0, order(0), sub(s)).start()
    for i in range(2):
        for j in range(3):
            weight_copy(i, j, core).start()
    token_load(order(2)).wait()
    norm_part(order(2))
    for s in range(SUBS):
        token_send(2, order(2), sub(s)).start()
    for n in (1, 3, 4, 5):
        token_load(order(n)).wait()

    norm_part(order(1))
    lax.fori_loop(3, PARTS, lambda n, carry: (norm_part(order(n)), carry)[1], 0)

    def slab_start(slab):
        return (slab_order[slab] * rows).astype(jnp.float32)

    def prepare():
        lane = lax.broadcasted_iota(jnp.int32, (1, HEAD_SIZE), 1)
        half = HEAD_SIZE // 2
        freqs = jnp.exp((lane % half).astype(jnp.float32) * (-2.0 * math.log(500000.0) / HEAD_SIZE))
        sign = jnp.where(lane < half, -1.0, 1.0)
        seg = segments[...]
        starts = [jnp.sum((seg < s).astype(jnp.float32)) for s in range(1, 4)]
        across = (lax.broadcasted_iota(jnp.int32, (1, lanes), 1) % part).astype(jnp.float32)

        def fill(p, carry):
            at = part_rows(p)
            first = (p * part).astype(jnp.float32)
            down = lax.broadcasted_iota(jnp.int32, (part, HEAD_SIZE), 0).astype(jnp.float32) + first
            for which, slab in ((0, t), (1, t_x)):
                angles = (down + slab_start(slab)) * freqs
                table[which, 0, at, :] = jnp.cos(angles)
                table[which, 1, at, :] = jnp.sin(angles) * sign
            place = across + first + slab_start(t)
            lowest = jnp.zeros_like(place)
            for start in starts:
                lowest = jnp.maximum(lowest, jnp.where(place >= start, start, 0.0))
            places[p] = place
            lows[p] = lowest
            return carry

        lax.fori_loop(0, PARTS, fill, 0)
        down = lax.broadcasted_iota(jnp.int32, (part, HEAD_SIZE), 0).astype(jnp.float32)
        for c in range(2):
            for x in range(2):
                first = (2 * c + x) * part
                kbase[first : first + part, :] = down + slab_start(2 * x + c)
        size = eye.shape[0]
        eye[...] = jnp.where(
            lax.broadcasted_iota(jnp.int32, (size, size), 0) == lax.broadcasted_iota(jnp.int32, (size, size), 1),
            1.0, 0.0,
        ).astype(jnp.bfloat16)
        peak[...] = jnp.full_like(peak, NEG)
        total[...] = jnp.zeros_like(total)
        acc[...] = jnp.zeros_like(acc)

    def own_product(s, k):
        columns = pl.ds(pl.multiple_of(x_index * near + k * depth, depth), depth)
        width = both

        def block(b, carry):
            at = pl.ds(pl.multiple_of(b * width, width), width)
            value = jnp.dot(normed[:, columns], wall[k, :, at], preferred_element_type=jnp.float32)
            own[:, at] = value if s == 0 else own[:, at] + value
            return carry

        lax.fori_loop(0, own.shape[1] // width, block, 0)

    def slot(n, p, s):
        k = sub(s)
        inner_send(n, p, k).wait_recv()

        @pl.when(to_outer(n))
        def _():
            outer_send(n, p, k).start()

        @pl.when(to_inner(n))
        def _():
            inner_send(n, p, k).start()

        @pl.when(n == 0)
        def _():
            for j in range(3):
                if s < 2:
                    weight_load(s, j).wait()
                else:
                    weight_copy(s - 2, j, 1 - core).wait_recv()
            own_product(s, k)

        value = jnp.dot(xrem[p, k], wall[k], preferred_element_type=jnp.float32)
        prem[...] = value if s == 0 else prem[...] + value

    def emit(n, p):
        keep[n] = prem[:, 0:both]
        skv[n, 0] = prem[:, 0:both].astype(jnp.bfloat16)
        skv[n, 1] = own[part_rows(p), 0:both].astype(jnp.bfloat16)
        kv_send(n).start()
        sq[n] = prem[:, both:].astype(jnp.bfloat16)
        q_send(n).start()

    def turned(values, which, at):
        swapped = pltpu.roll(values, HEAD_SIZE // 2, 1)
        return (values * table[which, 0, at, :] + swapped * table[which, 1, at, :]).astype(jnp.bfloat16)

    def finish_keys(n):
        at = part_rows(order(n))

        def place(values, which, x):
            into = pl.ds(pl.multiple_of(core * 2 * part + x * part, part), part)
            for head in range(kv_heads):
                columns = slice(head * HEAD_SIZE, (head + 1) * HEAD_SIZE)
                kv[n, into, columns] = turned(values[:, columns], which, at)
            kv[n, into, kv_cols:both] = values[:, kv_cols:both].astype(jnp.bfloat16)

        kv_send(n).wait_recv()
        place(own[at, 0:both] + rkv[n, 0].astype(jnp.float32), 0, x_index)
        place(rkv[n, 1].astype(jnp.float32) + keep[n], 1, 1 - x_index)
        mate_copy(n, core).start()

    def finish_queries(n):
        at = part_rows(order(n))
        q_send(n).wait_recv()
        for head in range(heads):
            low = both + head * HEAD_SIZE
            values = own[at, low : low + HEAD_SIZE] + rq[
                n, :, head * HEAD_SIZE : (head + 1) * HEAD_SIZE
            ].astype(jnp.float32)
            first = (head % group_width) * part
            qrot[n, head // group_width, first : first + part, :] = turned(values, 0, at)

    factor = (HEAD_SIZE ** (-0.5)) * math.log2(math.e)
    pairs = (((1,), (1,)), ((), ()))

    def update(i, j):
        offset = (order(j) * part).astype(jnp.float32)
        place = places[order(i)] - offset
        lowest = lows[order(i)] - offset
        where = jnp.concatenate([kbase[...]] * (lanes // HEAD_SIZE), axis=1)
        bias = jnp.where((where <= place) & (where >= lowest), 0.0, NEG)
        old = [peak[i, h] for h in range(kv_heads)]
        sums = [total[i, h] for h in range(kv_heads)]
        held = [acc[i, h] for h in range(kv_heads)]
        scores = [
            lax.dot_general(
                kv[j, :, h * HEAD_SIZE : (h + 1) * HEAD_SIZE], qrot[i, h], pairs,
                preferred_element_type=jnp.float32,
            ) + bias
            for h in range(kv_heads)
        ]
        new = [jnp.maximum(old[h], jnp.max(scores[h], axis=0, keepdims=True)) for h in range(kv_heads)]
        exps = [jnp.exp2((scores[h] - new[h]) * factor) for h in range(kv_heads)]
        mixed = [
            jnp.dot(
                vt[j, h * HEAD_SIZE : (h + 1) * HEAD_SIZE, :], exps[h].astype(jnp.bfloat16),
                preferred_element_type=jnp.float32,
            )
            for h in range(kv_heads)
        ]
        for h in range(kv_heads):
            fade = jnp.exp2((old[h] - new[h]) * factor)
            peak[i, h] = new[h]
            total[i, h] = sums[h] * fade + jnp.sum(exps[h], axis=0, keepdims=True)
            acc[i, h] = held[h] * fade + mixed[h]

    def finish(n):
        finish_keys(n)
        mate_copy(n, 1 - core).wait_recv()
        vt[n] = lax.dot_general(
            eye[...], kv[n, :, kv_cols:both], pairs, preferred_element_type=jnp.float32
        ).astype(jnp.bfloat16)

        def earlier(i, carry):
            update(i, n)
            return carry

        lax.fori_loop(0, n, earlier, 0)
        finish_queries(n)

        def fresh(j, carry):
            update(n, j)
            return carry

        lax.fori_loop(0, n + 1, fresh, 0)

    def step(n, carry):
        p = order(n)

        @pl.when(n < PARTS)
        def _():
            slot(n, p, 0)
            slot(n, p, 1)

        @pl.when(n == 1)
        def _():
            prepare()

        @pl.when(n >= LAG)
        def _():
            finish(2 * (n - LAG))

        @pl.when(n < PARTS)
        def _():
            slot(n, p, 2)

        @pl.when(n >= LAG)
        def _():
            finish(2 * (n - LAG) + 1)

        @pl.when(n < PARTS)
        def _():
            slot(n, p, 3)
            emit(n, p)

        return carry

    lax.fori_loop(0, PARTS + 1, step, 0)

    def close(n, carry):
        at = part_rows(order(n))
        for h in range(kv_heads):
            scaled = (acc[n, h] * (1.0 / total[n, h])).astype(jnp.bfloat16)
            upright = lax.dot_general(eye[...], scaled, pairs, preferred_element_type=jnp.float32)
            for member in range(group_width):
                low = (h * group_width + member) * HEAD_SIZE
                out[at, low : low + HEAD_SIZE] = upright[member * part : (member + 1) * part].astype(jnp.bfloat16)
        return carry

    lax.fori_loop(0, PARTS, close, 0)

    for i in range(2):
        for j in range(3):
            weight_copy(i, j, core).wait_send()

    def drain(n, carry):
        p = order(n)
        kv_send(n).wait_send()
        q_send(n).wait_send()
        mate_copy(n, core).wait_send()
        for k in range(SUBS):
            @pl.when((n == 0) | (n == 2))
            def _():
                token_send(n, p, k).wait_send()

            @pl.when(to_inner(n))
            def _():
                inner_send(n, p, k).wait_send()

            @pl.when(to_outer(n))
            def _():
                outer_send(n, p, k).wait_send()

        return carry

    lax.fori_loop(0, PARTS, drain, 0)


def local_fused(tokens, norm_gain, w_query, w_key, value_weight, slab_order, segment_ids):
    rows, width = tokens.shape
    shard_rows, query_cols = w_query.shape
    kv_cols = w_key.shape[1]
    kv_heads = kv_cols // HEAD_SIZE
    group_width = query_cols // kv_cols
    columns = query_cols + 2 * kv_cols
    part = rows // PARTS
    depth = shard_rows // 2
    lanes = group_width * part
    whole = pl.BlockSpec(memory_space=pltpu.VMEM)
    scalars = pl.BlockSpec(memory_space=pltpu.SMEM)
    hbm = pl.BlockSpec(memory_space=pl.ANY)
    half = jnp.bfloat16
    single = jnp.float32
    sem = pltpu.SemaphoreType.DMA
    return pl.pallas_call(
        fused_kernel,
        out_shape=jax.ShapeDtypeStruct((rows, query_cols), jnp.bfloat16),
        in_specs=[hbm, whole, hbm, hbm, hbm, scalars, whole],
        out_specs=whole,
        scratch_shapes=[
            pltpu.VMEM((SUBS, depth, columns), half),
            pltpu.VMEM((rows, width), half),
            pltpu.VMEM((1, width), single),
            pltpu.VMEM((rows, columns), single),
            pltpu.VMEM((part, columns), single),
            pltpu.VMEM((PARTS, SUBS, part, depth), half),
            pltpu.VMEM((PARTS, 2, part, 2 * kv_cols), half),
            pltpu.VMEM((PARTS, 2, part, 2 * kv_cols), half),
            pltpu.VMEM((PARTS, part, query_cols), half),
            pltpu.VMEM((PARTS, part, query_cols), half),
            pltpu.VMEM((PARTS, part, 2 * kv_cols), single),
            pltpu.VMEM((PARTS, kv_heads, lanes, HEAD_SIZE), half),
            pltpu.VMEM((PARTS, 4 * part, 2 * kv_cols), half),
            pltpu.VMEM((PARTS, kv_cols, 4 * part), half),
            pltpu.VMEM((2, 2, rows, HEAD_SIZE), single),
            pltpu.VMEM((PARTS, 1, lanes), single),
            pltpu.VMEM((PARTS, 1, lanes), single),
            pltpu.VMEM((4 * part, HEAD_SIZE), single),
            pltpu.VMEM((lanes, lanes), half),
            pltpu.VMEM((PARTS, kv_heads, 1, lanes), single),
            pltpu.VMEM((PARTS, kv_heads, 1, lanes), single),
            pltpu.VMEM((PARTS, kv_heads, HEAD_SIZE, lanes), single),
            sem((PARTS,)), sem((2, 3)), sem((2, 3)), sem((2, 3)),
            sem((2, SUBS)), sem((PARTS, SUBS)), sem((PARTS, SUBS)), sem((PARTS, SUBS)),
            sem((PARTS,)), sem((PARTS,)), sem((PARTS,)), sem((PARTS,)), sem((PARTS,)), sem((PARTS,)),
        ],
        compiler_params=pltpu.CompilerParams(
            collective_id=0, has_side_effects=True, vmem_limit_bytes=58 << 20
        ),
        cost_estimate=pl.CostEstimate(
            flops=2 * rows * width * columns, bytes_accessed=40 << 20, transcendentals=rows * 4 * rows * 8
        ),
    )(tokens, norm_gain, w_query, w_key, value_weight, slab_order, segment_ids)


def solution(mesh):
    small = mesh.shape["ctx"] == 4 and mesh.shape["groups"] == 2 and mesh.shape["mp"] == 4
    local = local_fused if small else local_plain
    return jax.shard_map(
        local,
        mesh=mesh,
        in_specs=(
            P(("groups", "ctx"), None),
            P(),
            P("ctx", "mp"),
            P("ctx", "mp"),
            P("ctx", "mp"),
            P("groups"),
            P("groups"),
        ),
        out_specs=P(("groups", "ctx"), "mp"),
        check_vma=False,
    )
```

```python
import functools
import math

import jax
import jax.numpy as jnp
from jax import lax
from jax.experimental import pallas as pl
from jax.experimental.pallas import tpu as pltpu
from jax.sharding import PartitionSpec as P

HEAD_SIZE = 128


def apply_rotary(values, positions, heads):
    width = values.shape[1] // heads
    half = width // 2
    freqs = jnp.exp(jnp.arange(half, dtype=jnp.float32) * (-2.0 * math.log(500000.0) / width))
    angles = positions.astype(jnp.float32)[:, None] * freqs[None, :]
    cosine = jnp.cos(angles)[:, None, :]
    sine = jnp.sin(angles)[:, None, :]
    shaped = values.reshape(values.shape[0], heads, width)
    first = shaped[..., :half]
    second = shaped[..., half:]
    turned = jnp.concatenate(
        [first * cosine - second * sine, second * cosine + first * sine], axis=-1
    )
    return turned.reshape(values.shape)


def local_plain(tokens, norm_gain, w_query, w_key, value_weight, slab_order, segment_ids):
    tok_rows = tokens.shape[0]
    device_slab = lax.axis_index("ctx")
    position_all = (
        slab_order[:, None] * tok_rows + jnp.arange(tok_rows, dtype=jnp.int32)[None, :]
    ).reshape(-1)
    segment_all = jnp.take(segment_ids, position_all)
    my_position = lax.dynamic_slice_in_dim(position_all, device_slab * tok_rows, tok_rows)
    my_segment = lax.dynamic_slice_in_dim(segment_all, device_slab * tok_rows, tok_rows)
    floats = tokens.astype(jnp.float32)
    inverse = lax.rsqrt(jnp.mean(floats * floats, axis=-1, keepdims=True) + 1e-05)
    normed = (floats * inverse * norm_gain.astype(jnp.float32)[None, :]).astype(jnp.bfloat16)
    query_cols = w_query.shape[1]
    key_cols = w_key.shape[1]
    query = jnp.dot(
        normed,
        lax.all_gather(w_query, "ctx", axis=0, tiled=True),
        preferred_element_type=jnp.float32,
    )
    key_projected = jnp.dot(
        normed, lax.all_gather(w_key, "ctx", axis=0, tiled=True), preferred_element_type=jnp.float32
    )
    value_proj = jnp.dot(
        normed,
        lax.all_gather(value_weight, "ctx", axis=0, tiled=True),
        preferred_element_type=jnp.float32,
    )
    head_size = HEAD_SIZE
    heads_here = query_cols // head_size
    kv_here = key_cols // head_size
    group_width = heads_here // kv_here
    query_rot = (
        apply_rotary(query, my_position, heads_here)
        .astype(jnp.bfloat16)
        .reshape(tok_rows, kv_here, group_width, head_size)
    )
    key_rotary = apply_rotary(key_projected, my_position, kv_here).astype(jnp.bfloat16)
    value_b = value_proj.astype(jnp.bfloat16)
    scale = head_size ** (-0.5)
    start_state = (
        jnp.full((kv_here, group_width, tok_rows), -1e30, jnp.float32),
        jnp.zeros((kv_here, group_width, tok_rows), jnp.float32),
        jnp.zeros((kv_here, group_width, tok_rows, head_size), jnp.float32),
    )
    state = start_state
    key_piece = lax.all_gather(key_rotary, "ctx", axis=0, tiled=True)
    value_piece = lax.all_gather(value_b, "ctx", axis=0, tiled=True)
    piece_rows = key_piece.shape[0]
    block_rows = math.gcd(piece_rows, 1024)
    block_count = piece_rows // block_rows
    key_blocks = key_piece.reshape(block_count, block_rows, kv_here, head_size)
    value_blocks = value_piece.reshape(block_count, block_rows, kv_here, head_size)
    key_positions = position_all.reshape(block_count, block_rows)
    key_segments = segment_all.reshape(block_count, block_rows)

    def advance(inner, item):
        key_block, value_block, block_positions, block_segments = item
        allowed = (block_positions[None, :] <= my_position[:, None]) & (
            block_segments[None, :] == my_segment[:, None]
        )
        running_max, running_sum, running_acc = inner
        scores = (
            jnp.einsum("tkgd,nkd->kgtn", query_rot, key_block, preferred_element_type=jnp.float32)
            * scale
        )
        scores = jnp.where(allowed[None, None], scores, -1e30)
        new_max = jnp.maximum(running_max, jnp.max(scores, axis=-1))
        exps = jnp.where(allowed[None, None], jnp.exp(scores - new_max[..., None]), 0.0)
        factor = jnp.exp(running_max - new_max)
        new_sum = running_sum * factor + jnp.sum(exps, axis=-1)
        new_acc = running_acc * factor[..., None] + jnp.einsum(
            "kgtn,nkd->kgtd",
            exps.astype(jnp.bfloat16),
            value_block,
            preferred_element_type=jnp.float32,
        )
        inner = (new_max, new_sum, new_acc)
        return (inner, None)

    state, _ = lax.scan(advance, state, (key_blocks, value_blocks, key_positions, key_segments))
    final_max, final_sum, final_acc = state
    mixed = final_acc / final_sum[..., None]
    return (
        jnp.transpose(mixed, (2, 0, 1, 3))
        .reshape(tok_rows, heads_here * head_size)
        .astype(jnp.bfloat16)
    )


NEG = -1e30
PARTS = 6
SUBS = 4


def fused_kernel(
    tokens, gain, w_query, w_key, w_value, slab_order, segments, out,
    wall, normed, gain_flat, gain_row, segment_row, slabs, own, prem, xrem, skv, rkv, sq, rq, keep, qrot, kv, vt,
    table, places, lows, kbase, eye, peak, total, acc, staged,
    tsem, ssem, wsem, ws, wr, xs, ins, outs, xr, kvs, kvr, qs, qr, cs, cr, osem,
):
    g = lax.axis_index("groups")
    t = lax.axis_index("ctx")
    m = lax.axis_index("mp")
    x_index = t // 2
    core = t % 2
    t_core = x_index * 2 + (1 - core)
    t_x = (1 - x_index) * 2 + core
    middle = (m == 1) | (m == 2)
    core_dev = (g, t_core, m)
    x_dev = (g, t_x, m)
    inner_dev = (g, t, 1 + m % 2)
    outer_dev = (g, t, 3 * (m // 2))
    rows = tokens.shape[0]
    part = rows // PARTS
    depth = wall.shape[1]
    near = depth * SUBS
    kv_cols = w_key.shape[1]
    kv_heads = kv_cols // HEAD_SIZE
    both = 2 * kv_cols
    heads = w_query.shape[1] // HEAD_SIZE
    group_width = heads // kv_heads
    keys = 4 * part
    lanes = group_width * part

    def order(n):
        high = m // 2
        side = m + high * (3 - 2 * m)
        later = n // 3
        end = (2 * n) % 5 + 5 * (n // 5)
        mid = ((n % 3) * (1 + later) + 2 * (1 - later)) % 3 + 3 * later
        p = end * (1 - side) + mid * side
        return p + high * (5 - 2 * p)

    def part_rows(p):
        return pl.ds(pl.multiple_of(p * part, part), part)

    def remote(src, dst, send, recv, dev):
        return pltpu.make_async_remote_copy(
            src_ref=src, dst_ref=dst, send_sem=send, recv_sem=recv,
            device_id=dev, device_id_type=pl.DeviceIdType.MESH,
        )

    def sub(s):
        return (2 * core + s) % SUBS

    def token_load(p):
        return pltpu.make_async_copy(tokens.at[part_rows(p), :], normed.at[part_rows(p), :], tsem.at[p])

    sources = (
        (w_key, pl.ds(0, kv_cols)),
        (w_value, pl.ds(kv_cols, kv_cols)),
        (w_query, pl.ds(both, heads * HEAD_SIZE)),
    )

    def weight_load(i, j):
        source, columns = sources[j]
        return pltpu.make_async_copy(
            source.at[pl.ds(i * depth, depth), :], wall.at[2 * core + i, :, columns], wsem.at[i, j]
        )

    def weight_copy(i, j, c):
        source, columns = sources[j]
        return remote(
            source.at[pl.ds(i * depth, depth), :], wall.at[2 * c + i, :, columns],
            ws.at[i, j], wr.at[i, j], core_dev,
        )

    def token_send(n, p, k):
        columns = pl.ds(pl.multiple_of((1 - x_index) * near + k * depth, depth), depth)
        return remote(normed.at[part_rows(p), columns], xrem.at[p, k], xs.at[n // 2, k], xr.at[p, k], x_dev)

    def inner_send(n, p, k):
        return remote(xrem.at[p, k], xrem.at[p, k], ins.at[n, k], xr.at[p, k], inner_dev)

    def outer_send(n, p, k):
        return remote(xrem.at[p, k], xrem.at[p, k], outs.at[n, k], xr.at[p, k], outer_dev)

    def to_inner(n):
        return (n == 0) | (middle & (n <= 2))

    def to_outer(n):
        return middle & (n != 1) & (n != 5)

    def own_send(n):
        return remote(skv.at[n, 1], rkv.at[n, 1], kvs.at[n, 1], kvr.at[n, 1], x_dev)

    def kv_send(n):
        return remote(skv.at[n, 0], rkv.at[n, 0], kvs.at[n, 0], kvr.at[n, 0], x_dev)

    def q_send(n):
        return remote(sq.at[n], rq.at[n], qs.at[n], qr.at[n], x_dev)

    def out_copy(n):
        at = part_rows(order(n))
        return pltpu.make_async_copy(staged.at[at, :], out.at[at, :], osem.at[n])

    def mate_copy(n, c):
        view = kv.at[n, pl.ds(pl.multiple_of(c * 2 * part, 2 * part), 2 * part), :]
        return remote(view, view, cs.at[n], cr.at[n], core_dev)

    small_loads = (
        pltpu.make_async_copy(gain, gain_flat, ssem.at[0]),
        pltpu.make_async_copy(slab_order, slabs, ssem.at[1]),
        pltpu.make_async_copy(segments, segment_row, ssem.at[2]),
    )
    barrier = pltpu.get_barrier_semaphore()
    for dev in (x_dev, inner_dev, core_dev):
        pl.semaphore_signal(barrier, inc=1, device_id=dev, device_id_type=pl.DeviceIdType.MESH)

    @pl.when(middle)
    def _():
        pl.semaphore_signal(barrier, inc=1, device_id=outer_dev, device_id_type=pl.DeviceIdType.MESH)

    small_loads[0].start()
    for n in (0, 2, 1, 3, 4, 5):
        token_load(order(n)).start()
        if n == 0:
            small_loads[1].start()
            small_loads[2].start()
            for i in range(2):
                for j in range(3):
                    weight_load(i, j).start()
    small_loads[0].wait()
    gain_row[...] = gain_flat[...].astype(jnp.float32).reshape(1, gain_flat.shape[0])

    def norm_part(p):
        def norm_rows(i, carry):
            at = pl.ds(pl.multiple_of(p * part + i * 16, 16), 16)
            floats = normed[at, :].astype(jnp.float32)
            inverse = lax.rsqrt(jnp.mean(floats * floats, axis=-1, keepdims=True) + 1e-05)
            normed[at, :] = (floats * inverse * gain_row[...]).astype(jnp.bfloat16)
            return carry

        lax.fori_loop(0, part // 16, norm_rows, 0)

    token_load(order(0)).wait()
    norm_part(order(0))

    @pl.when(middle)
    def _():
        pl.semaphore_wait(barrier, 4)

    @pl.when(jnp.logical_not(middle))
    def _():
        pl.semaphore_wait(barrier, 3)

    for s in range(SUBS):
        token_send(0, order(0), sub(s)).start()
    for i in range(2):
        for j in range(3):
            weight_copy(i, j, core).start()
    token_load(order(2)).wait()
    norm_part(order(2))
    for s in range(SUBS):
        token_send(2, order(2), sub(s)).start()
    for n in (1, 3, 4, 5):
        token_load(order(n)).wait()

    norm_part(order(1))
    lax.fori_loop(3, PARTS, lambda n, carry: (norm_part(order(n)), carry)[1], 0)

    def slab_start(slab):
        return (slabs[slab] * rows).astype(jnp.float32)

    def prepare():
        small_loads[1].wait()
        small_loads[2].wait()
        lane = lax.broadcasted_iota(jnp.int32, (1, HEAD_SIZE), 1)
        half = HEAD_SIZE // 2
        freqs = jnp.exp((lane % half).astype(jnp.float32) * (-2.0 * math.log(500000.0) / HEAD_SIZE))
        sign = jnp.where(lane < half, -1.0, 1.0)
        seg = segment_row[...]
        starts = [jnp.sum((seg < s).astype(jnp.float32)) for s in range(1, 4)]
        across = (lax.broadcasted_iota(jnp.int32, (1, lanes), 1) % part).astype(jnp.float32)

        def fill(p, carry):
            at = part_rows(p)
            first = (p * part).astype(jnp.float32)
            down = lax.broadcasted_iota(jnp.int32, (part, HEAD_SIZE), 0).astype(jnp.float32) + first
            for which, slab in ((0, t), (1, t_x)):
                angles = (down + slab_start(slab)) * freqs
                table[which, 0, at, :] = jnp.cos(angles)
                table[which, 1, at, :] = jnp.sin(angles) * sign
            place = across + first + slab_start(t)
            lowest = jnp.zeros_like(place)
            for start in starts:
                lowest = jnp.maximum(lowest, jnp.where(place >= start, start, 0.0))
            places[p] = place
            lows[p] = lowest
            return carry

        lax.fori_loop(0, PARTS, fill, 0)
        down = lax.broadcasted_iota(jnp.int32, (part, HEAD_SIZE), 0).astype(jnp.float32)
        for c in range(2):
            for x in range(2):
                first = (2 * c + x) * part
                kbase[first : first + part, :] = down + slab_start(2 * x + c)
        size = eye.shape[0]
        eye[...] = jnp.where(
            lax.broadcasted_iota(jnp.int32, (size, size), 0) == lax.broadcasted_iota(jnp.int32, (size, size), 1),
            1.0, 0.0,
        ).astype(jnp.bfloat16)

    def own_product(s):
        k = sub(s)
        columns = pl.ds(pl.multiple_of(x_index * near + k * depth, depth), depth)
        width = both

        def block(b, carry):
            at = pl.ds(pl.multiple_of(b * width, width), width)
            own[:, at] = own[:, at] + jnp.dot(
                normed[:, columns], wall[k, :, at], preferred_element_type=jnp.float32
            )
            return carry

        lax.fori_loop(0, own.shape[1] // width, block, 0)

    def relay(n, s):
        p = order(n)
        k = sub(s)
        inner_send(n, p, k).wait_recv()

        @pl.when(to_outer(n))
        def _():
            outer_send(n, p, k).start()

        @pl.when(to_inner(n))
        def _():
            inner_send(n, p, k).start()

    def send_own(n):
        skv[n, 1] = own[part_rows(order(n)), 0:both].astype(jnp.bfloat16)
        own_send(n).start()

    def emit(n, at):
        keep[n] = prem[at, 0:both]
        skv[n, 0] = prem[at, 0:both].astype(jnp.bfloat16)
        kv_send(n).start()
        sq[n] = prem[at, both:].astype(jnp.bfloat16)
        q_send(n).start()

    def turned(values, which, at):
        swapped = pltpu.roll(values, HEAD_SIZE // 2, 1)
        return (values * table[which, 0, at, :] + swapped * table[which, 1, at, :]).astype(jnp.bfloat16)

    def finish_keys(n):
        at = part_rows(order(n))

        def place(values, which, x):
            into = pl.ds(pl.multiple_of(core * 2 * part + x * part, part), part)
            for head in range(kv_heads):
                columns = slice(head * HEAD_SIZE, (head + 1) * HEAD_SIZE)
                kv[n, into, columns] = turned(values[:, columns], which, at)
            kv[n, into, kv_cols:both] = values[:, kv_cols:both].astype(jnp.bfloat16)

        own_send(n).wait_recv()
        kv_send(n).wait_recv()
        place(own[at, 0:both] + rkv[n, 0].astype(jnp.float32), 0, x_index)
        place(rkv[n, 1].astype(jnp.float32) + keep[n], 1, 1 - x_index)
        mate_copy(n, core).start()

    def finish_queries(n):
        at = part_rows(order(n))
        q_send(n).wait_recv()
        for head in range(heads):
            low = both + head * HEAD_SIZE
            values = own[at, low : low + HEAD_SIZE] + rq[
                n, :, head * HEAD_SIZE : (head + 1) * HEAD_SIZE
            ].astype(jnp.float32)
            first = (head % group_width) * part
            qrot[n, head // group_width, first : first + part, :] = turned(values, 0, at)

    factor = (HEAD_SIZE ** (-0.5)) * math.log2(math.e)
    pairs = (((1,), (1,)), ((), ()))

    def finish(n):
        finish_keys(n)
        finish_queries(n)

    def take(n):
        mate_copy(n, 1 - core).wait_recv()
        vt[n] = lax.dot_general(
            eye[...], kv[n, :, kv_cols:both], pairs, preferred_element_type=jnp.float32
        ).astype(jnp.bfloat16)

    def masked(i, j, where):
        offset = (order(j) * part).astype(jnp.float32)
        p = order(i)
        inside = (where <= places[p] - offset) & (where >= lows[p] - offset)
        bias = jnp.where(inside, 0.0, NEG)
        return [
            lax.dot_general(
                kv[j, :, h * HEAD_SIZE : (h + 1) * HEAD_SIZE], qrot[i, h], pairs,
                preferred_element_type=jnp.float32,
            ) + bias
            for h in range(kv_heads)
        ]

    def wide_base():
        return jnp.concatenate([kbase[...]] * (lanes // HEAD_SIZE), axis=1)

    def fresh(i, count):
        where = wide_base()
        blocks = [masked(i, j, where) for j in range(count)]
        for h in range(kv_heads):
            highest = blocks[0][h]
            for j in range(1, count):
                highest = jnp.maximum(highest, blocks[j][h])
            top = jnp.max(highest, axis=0, keepdims=True)
            exps = [jnp.exp2((blocks[j][h] - top) * factor) for j in range(count)]
            summed = exps[0]
            for j in range(1, count):
                summed = summed + exps[j]
            peak[i, h] = top
            total[i, h] = jnp.sum(summed, axis=0, keepdims=True)
            acc[i, h] = jnp.dot(
                jnp.concatenate([vt[j, h * HEAD_SIZE : (h + 1) * HEAD_SIZE, :] for j in range(count)], axis=1),
                jnp.concatenate([e.astype(jnp.bfloat16) for e in exps], axis=0),
                preferred_element_type=jnp.float32,
            )

    def earlier(j, count):
        where = wide_base()
        chains = [(i, h) for i in range(count) for h in range(kv_heads)]
        old = [peak[i, h] for i, h in chains]
        sums = [total[i, h] for i, h in chains]
        held = [acc[i, h] for i, h in chains]
        scores = [s for i in range(count) for s in masked(i, j, where)]
        new = [jnp.maximum(o, jnp.max(s, axis=0, keepdims=True)) for o, s in zip(old, scores)]
        exps = [jnp.exp2((s - top) * factor) for s, top in zip(scores, new)]
        mixed = [
            jnp.dot(
                vt[j, h * HEAD_SIZE : (h + 1) * HEAD_SIZE, :], e.astype(jnp.bfloat16),
                preferred_element_type=jnp.float32,
            )
            for (i, h), e in zip(chains, exps)
        ]
        for c, (i, h) in enumerate(chains):
            fade = jnp.exp2((old[c] - new[c]) * factor)
            peak[i, h] = new[c]
            total[i, h] = sums[c] * fade + jnp.sum(exps[c], axis=0, keepdims=True)
            acc[i, h] = held[c] * fade + mixed[c]

    prepare()
    own[...] = jnp.zeros_like(own)

    def first(s, carry):
        relay(0, s)
        for j in range(3):
            @pl.when(s < 2)
            def _():
                weight_load(s, j).wait()

            @pl.when(s >= 2)
            def _():
                weight_copy(s - 2, j, 1 - core).wait_recv()

        own_product(s)
        return carry

    lax.fori_loop(0, SUBS, first, 0)
    send_own(0)
    send_own(1)

    def pair(n, s, carry):
        k = sub(s)
        prem[...] = prem[...] + jnp.dot(
            jnp.concatenate([xrem[order(n), k], xrem[order(n + 1), k]], axis=0), wall[k],
            preferred_element_type=jnp.float32,
        )
        return carry

    prem[...] = jnp.zeros_like(prem)
    for s in range(3):
        relay(1, s)
    relay(2, 0)
    relay(1, 3)
    lax.fori_loop(0, 2, functools.partial(pair, 0), 0)
    relay(2, 1)
    lax.fori_loop(2, SUBS, functools.partial(pair, 0), 0)
    emit(0, slice(0, part))
    emit(1, slice(part, 2 * part))
    send_own(2)
    send_own(3)
    relay(2, 2)
    relay(2, 3)
    prem[...] = jnp.zeros_like(prem)

    def third(s, carry):
        relay(3, s)
        return pair(2, s, carry)

    lax.fori_loop(0, SUBS, third, 0)
    emit(2, slice(0, part))
    emit(3, slice(part, 2 * part))
    send_own(4)
    send_own(5)

    def single(u, carry):
        n = 4 + u // SUBS
        s = u % SUBS
        relay(n, s)
        k = sub(s)

        @pl.when(s == 0)
        def _():
            prem[0:part] = jnp.zeros((part, prem.shape[1]), jnp.float32)

        prem[0:part] = prem[0:part] + jnp.dot(xrem[order(n), k], wall[k], preferred_element_type=jnp.float32)

        @pl.when(s == SUBS - 1)
        def _():
            emit(n, slice(0, part))

        @pl.when(s < 2)
        def _():
            done = 2 * (u // SUBS) + s
            finish(done)
            take(done)

        @pl.when(u == SUBS)
        def _():
            lax.fori_loop(0, 3, lambda i, c: (fresh(i, 3), c)[1], 0)

        @pl.when(u == SUBS + 1)
        def _():
            earlier(3, 3)
            fresh(3, 4)

        return carry

    lax.fori_loop(0, 2 * SUBS, single, 0)
    finish(4)
    take(4)
    earlier(4, 4)
    fresh(4, 5)
    finish_keys(5)
    take(5)
    earlier(5, 5)

    def close(n, carry):
        at = part_rows(order(n))
        for h in range(kv_heads):
            scaled = (acc[n, h] * (1.0 / total[n, h])).astype(jnp.bfloat16)
            upright = lax.dot_general(eye[...], scaled, pairs, preferred_element_type=jnp.float32)
            for member in range(group_width):
                low = (h * group_width + member) * HEAD_SIZE
                staged[at, low : low + HEAD_SIZE] = upright[member * part : (member + 1) * part].astype(jnp.bfloat16)
        out_copy(n).start()
        return carry

    lax.fori_loop(0, PARTS - 1, close, 0)
    finish_queries(5)
    fresh(5, 6)
    close(5, 0)

    for i in range(2):
        for j in range(3):
            weight_copy(i, j, core).wait_send()

    def drain(n, carry):
        p = order(n)
        own_send(n).wait_send()
        kv_send(n).wait_send()
        q_send(n).wait_send()
        mate_copy(n, core).wait_send()
        for k in range(SUBS):
            @pl.when((n == 0) | (n == 2))
            def _():
                token_send(n, p, k).wait_send()

            @pl.when(to_inner(n))
            def _():
                inner_send(n, p, k).wait_send()

            @pl.when(to_outer(n))
            def _():
                outer_send(n, p, k).wait_send()

        return carry

    lax.fori_loop(0, PARTS, drain, 0)
    lax.fori_loop(0, PARTS, lambda n, carry: (out_copy(n).wait(), carry)[1], 0)


def local_fused(tokens, norm_gain, w_query, w_key, value_weight, slab_order, segment_ids):
    rows, width = tokens.shape
    shard_rows, query_cols = w_query.shape
    kv_cols = w_key.shape[1]
    kv_heads = kv_cols // HEAD_SIZE
    group_width = query_cols // kv_cols
    columns = query_cols + 2 * kv_cols
    part = rows // PARTS
    depth = shard_rows // 2
    lanes = group_width * part
    hbm = pl.BlockSpec(memory_space=pl.ANY)
    half = jnp.bfloat16
    single = jnp.float32
    sem = pltpu.SemaphoreType.DMA
    return pl.pallas_call(
        fused_kernel,
        out_shape=jax.ShapeDtypeStruct((rows, query_cols), jnp.bfloat16),
        in_specs=[hbm] * 7,
        out_specs=hbm,
        scratch_shapes=[
            pltpu.VMEM((SUBS, depth, columns), half),
            pltpu.VMEM((rows, width), half),
            pltpu.VMEM((width,), half),
            pltpu.VMEM((1, width), single),
            pltpu.VMEM(segment_ids.shape, jnp.int32),
            pltpu.SMEM(slab_order.shape, jnp.int32),
            pltpu.VMEM((rows, columns), single),
            pltpu.VMEM((2 * part, columns), single),
            pltpu.VMEM((PARTS, SUBS, part, depth), half),
            pltpu.VMEM((PARTS, 2, part, 2 * kv_cols), half),
            pltpu.VMEM((PARTS, 2, part, 2 * kv_cols), half),
            pltpu.VMEM((PARTS, part, query_cols), half),
            pltpu.VMEM((PARTS, part, query_cols), half),
            pltpu.VMEM((PARTS, part, 2 * kv_cols), single),
            pltpu.VMEM((PARTS, kv_heads, lanes, HEAD_SIZE), half),
            pltpu.VMEM((PARTS, 4 * part, 2 * kv_cols), half),
            pltpu.VMEM((PARTS, kv_cols, 4 * part), half),
            pltpu.VMEM((2, 2, rows, HEAD_SIZE), single),
            pltpu.VMEM((PARTS, 1, lanes), single),
            pltpu.VMEM((PARTS, 1, lanes), single),
            pltpu.VMEM((4 * part, HEAD_SIZE), single),
            pltpu.VMEM((lanes, lanes), half),
            pltpu.VMEM((PARTS, kv_heads, 1, lanes), single),
            pltpu.VMEM((PARTS, kv_heads, 1, lanes), single),
            pltpu.VMEM((PARTS, kv_heads, HEAD_SIZE, lanes), single),
            pltpu.VMEM((rows, query_cols), half),
            sem((PARTS,)), sem((3,)), sem((2, 3)), sem((2, 3)), sem((2, 3)),
            sem((2, SUBS)), sem((PARTS, SUBS)), sem((PARTS, SUBS)), sem((PARTS, SUBS)),
            sem((PARTS, 2)), sem((PARTS, 2)), sem((PARTS,)), sem((PARTS,)), sem((PARTS,)), sem((PARTS,)), sem((PARTS,)),
        ],
        compiler_params=pltpu.CompilerParams(
            collective_id=0, has_side_effects=True, vmem_limit_bytes=58 << 20
        ),
        cost_estimate=pl.CostEstimate(
            flops=2 * rows * width * columns, bytes_accessed=40 << 20, transcendentals=rows * 4 * rows * 8
        ),
    )(tokens, norm_gain, w_query, w_key, value_weight, slab_order, segment_ids)


def solution(mesh):
    small = mesh.shape["ctx"] == 4 and mesh.shape["groups"] == 2 and mesh.shape["mp"] == 4
    local = local_fused if small else local_plain
    return jax.shard_map(
        local,
        mesh=mesh,
        in_specs=(
            P(("groups", "ctx"), None),
            P(),
            P("ctx", "mp"),
            P("ctx", "mp"),
            P("ctx", "mp"),
            P("groups"),
            P("groups"),
        ),
        out_specs=P(("groups", "ctx"), "mp"),
        check_vma=False,
    )
```

```python
import functools
import math

import jax
import jax.numpy as jnp
from jax import lax
from jax.experimental import pallas as pl
from jax.experimental.pallas import tpu as pltpu
from jax.sharding import PartitionSpec as P

HEAD_SIZE = 128


def apply_rotary(values, positions, heads):
    width = values.shape[1] // heads
    half = width // 2
    freqs = jnp.exp(jnp.arange(half, dtype=jnp.float32) * (-2.0 * math.log(500000.0) / width))
    angles = positions.astype(jnp.float32)[:, None] * freqs[None, :]
    cosine = jnp.cos(angles)[:, None, :]
    sine = jnp.sin(angles)[:, None, :]
    shaped = values.reshape(values.shape[0], heads, width)
    first = shaped[..., :half]
    second = shaped[..., half:]
    turned = jnp.concatenate(
        [first * cosine - second * sine, second * cosine + first * sine], axis=-1
    )
    return turned.reshape(values.shape)


def local_plain(tokens, norm_gain, w_query, w_key, value_weight, slab_order, segment_ids):
    tok_rows = tokens.shape[0]
    device_slab = lax.axis_index("ctx")
    position_all = (
        slab_order[:, None] * tok_rows + jnp.arange(tok_rows, dtype=jnp.int32)[None, :]
    ).reshape(-1)
    segment_all = jnp.take(segment_ids, position_all)
    my_position = lax.dynamic_slice_in_dim(position_all, device_slab * tok_rows, tok_rows)
    my_segment = lax.dynamic_slice_in_dim(segment_all, device_slab * tok_rows, tok_rows)
    floats = tokens.astype(jnp.float32)
    inverse = lax.rsqrt(jnp.mean(floats * floats, axis=-1, keepdims=True) + 1e-05)
    normed = (floats * inverse * norm_gain.astype(jnp.float32)[None, :]).astype(jnp.bfloat16)
    query_cols = w_query.shape[1]
    key_cols = w_key.shape[1]
    query = jnp.dot(
        normed,
        lax.all_gather(w_query, "ctx", axis=0, tiled=True),
        preferred_element_type=jnp.float32,
    )
    key_projected = jnp.dot(
        normed, lax.all_gather(w_key, "ctx", axis=0, tiled=True), preferred_element_type=jnp.float32
    )
    value_proj = jnp.dot(
        normed,
        lax.all_gather(value_weight, "ctx", axis=0, tiled=True),
        preferred_element_type=jnp.float32,
    )
    head_size = HEAD_SIZE
    heads_here = query_cols // head_size
    kv_here = key_cols // head_size
    group_width = heads_here // kv_here
    query_rot = (
        apply_rotary(query, my_position, heads_here)
        .astype(jnp.bfloat16)
        .reshape(tok_rows, kv_here, group_width, head_size)
    )
    key_rotary = apply_rotary(key_projected, my_position, kv_here).astype(jnp.bfloat16)
    value_b = value_proj.astype(jnp.bfloat16)
    scale = head_size ** (-0.5)
    start_state = (
        jnp.full((kv_here, group_width, tok_rows), -1e30, jnp.float32),
        jnp.zeros((kv_here, group_width, tok_rows), jnp.float32),
        jnp.zeros((kv_here, group_width, tok_rows, head_size), jnp.float32),
    )
    state = start_state
    key_piece = lax.all_gather(key_rotary, "ctx", axis=0, tiled=True)
    value_piece = lax.all_gather(value_b, "ctx", axis=0, tiled=True)
    piece_rows = key_piece.shape[0]
    block_rows = math.gcd(piece_rows, 1024)
    block_count = piece_rows // block_rows
    key_blocks = key_piece.reshape(block_count, block_rows, kv_here, head_size)
    value_blocks = value_piece.reshape(block_count, block_rows, kv_here, head_size)
    key_positions = position_all.reshape(block_count, block_rows)
    key_segments = segment_all.reshape(block_count, block_rows)

    def advance(inner, item):
        key_block, value_block, block_positions, block_segments = item
        allowed = (block_positions[None, :] <= my_position[:, None]) & (
            block_segments[None, :] == my_segment[:, None]
        )
        running_max, running_sum, running_acc = inner
        scores = (
            jnp.einsum("tkgd,nkd->kgtn", query_rot, key_block, preferred_element_type=jnp.float32)
            * scale
        )
        scores = jnp.where(allowed[None, None], scores, -1e30)
        new_max = jnp.maximum(running_max, jnp.max(scores, axis=-1))
        exps = jnp.where(allowed[None, None], jnp.exp(scores - new_max[..., None]), 0.0)
        factor = jnp.exp(running_max - new_max)
        new_sum = running_sum * factor + jnp.sum(exps, axis=-1)
        new_acc = running_acc * factor[..., None] + jnp.einsum(
            "kgtn,nkd->kgtd",
            exps.astype(jnp.bfloat16),
            value_block,
            preferred_element_type=jnp.float32,
        )
        inner = (new_max, new_sum, new_acc)
        return (inner, None)

    state, _ = lax.scan(advance, state, (key_blocks, value_blocks, key_positions, key_segments))
    final_max, final_sum, final_acc = state
    mixed = final_acc / final_sum[..., None]
    return (
        jnp.transpose(mixed, (2, 0, 1, 3))
        .reshape(tok_rows, heads_here * head_size)
        .astype(jnp.bfloat16)
    )


NEG = -1e30
PARTS = 6
SUBS = 4


def fused_kernel(
    tokens, gain, w_query, w_key, w_value, slab_order, segments, out,
    wall, normed, gain_flat, gain_row, segment_row, slabs, own, prem, xrem, skv, rkv, sq, rq, keep, qrot, kv, vt,
    table, places, lows, kbase, eye, peak, total, acc,
    tsem, ssem, wsem, ws, wr, xs, ins, outs, xr, kvs, kvr, qs, qr, cs, cr,
):
    g = lax.axis_index("groups")
    t = lax.axis_index("ctx")
    m = lax.axis_index("mp")
    x_index = t // 2
    core = t % 2
    t_core = x_index * 2 + (1 - core)
    t_x = (1 - x_index) * 2 + core
    middle = (m == 1) | (m == 2)
    core_dev = (g, t_core, m)
    x_dev = (g, t_x, m)
    inner_dev = (g, t, 1 + m % 2)
    outer_dev = (g, t, 3 * (m // 2))
    rows = tokens.shape[0]
    part = rows // PARTS
    depth = wall.shape[1]
    near = depth * SUBS
    kv_cols = w_key.shape[1]
    kv_heads = kv_cols // HEAD_SIZE
    both = 2 * kv_cols
    heads = w_query.shape[1] // HEAD_SIZE
    group_width = heads // kv_heads
    keys = 4 * part
    lanes = group_width * part

    def order(n):
        high = m // 2
        side = m + high * (3 - 2 * m)
        later = n // 3
        end = (2 * n) % 5 + 5 * (n // 5)
        mid = ((n % 3) * (1 + later) + 2 * (1 - later)) % 3 + 3 * later
        p = end * (1 - side) + mid * side
        return p + high * (5 - 2 * p)

    def part_rows(p):
        return pl.ds(pl.multiple_of(p * part, part), part)

    def remote(src, dst, send, recv, dev):
        return pltpu.make_async_remote_copy(
            src_ref=src, dst_ref=dst, send_sem=send, recv_sem=recv,
            device_id=dev, device_id_type=pl.DeviceIdType.MESH,
        )

    def sub(s):
        return (2 * core + s) % SUBS

    def token_load(p):
        return pltpu.make_async_copy(tokens.at[part_rows(p), :], normed.at[part_rows(p), :], tsem.at[p])

    sources = (
        (w_key, pl.ds(0, kv_cols)),
        (w_value, pl.ds(kv_cols, kv_cols)),
        (w_query, pl.ds(both, heads * HEAD_SIZE)),
    )

    def weight_load(i, j):
        source, columns = sources[j]
        return pltpu.make_async_copy(
            source.at[pl.ds(i * depth, depth), :], wall.at[2 * core + i, :, columns], wsem.at[i, j]
        )

    def weight_copy(i, j, c):
        source, columns = sources[j]
        return remote(
            source.at[pl.ds(i * depth, depth), :], wall.at[2 * c + i, :, columns],
            ws.at[i, j], wr.at[i, j], core_dev,
        )

    def token_send(n, p, k):
        columns = pl.ds(pl.multiple_of((1 - x_index) * near + k * depth, depth), depth)
        return remote(normed.at[part_rows(p), columns], xrem.at[p, k], xs.at[n // 2, k], xr.at[p, k], x_dev)

    def inner_send(n, p, k):
        return remote(xrem.at[p, k], xrem.at[p, k], ins.at[n, k], xr.at[p, k], inner_dev)

    def outer_send(n, p, k):
        return remote(xrem.at[p, k], xrem.at[p, k], outs.at[n, k], xr.at[p, k], outer_dev)

    def to_inner(n):
        return (n == 0) | (middle & (n <= 2))

    def to_outer(n):
        return middle & (n != 1) & (n != 5)

    def own_send(n):
        return remote(skv.at[n, 1], rkv.at[n, 1], kvs.at[n, 1], kvr.at[n, 1], x_dev)

    def kv_send(n):
        return remote(skv.at[n, 0], rkv.at[n, 0], kvs.at[n, 0], kvr.at[n, 0], x_dev)

    def q_send(n):
        return remote(sq.at[n], rq.at[n], qs.at[n], qr.at[n], x_dev)

    def mate_copy(n, c):
        view = kv.at[n, pl.ds(pl.multiple_of(c * 2 * part, 2 * part), 2 * part), :]
        return remote(view, view, cs.at[n], cr.at[n], core_dev)

    small_loads = (
        pltpu.make_async_copy(gain, gain_flat, ssem.at[0]),
        pltpu.make_async_copy(slab_order, slabs, ssem.at[1]),
        pltpu.make_async_copy(segments, segment_row, ssem.at[2]),
    )
    barrier = pltpu.get_barrier_semaphore()
    for dev in (x_dev, inner_dev, core_dev):
        pl.semaphore_signal(barrier, inc=1, device_id=dev, device_id_type=pl.DeviceIdType.MESH)

    @pl.when(middle)
    def _():
        pl.semaphore_signal(barrier, inc=1, device_id=outer_dev, device_id_type=pl.DeviceIdType.MESH)

    small_loads[0].start()
    for n in (0, 2, 1, 3, 4, 5):
        token_load(order(n)).start()
        if n == 0:
            small_loads[1].start()
            small_loads[2].start()
            for i in range(2):
                for j in range(3):
                    weight_load(i, j).start()
    small_loads[0].wait()
    gain_row[...] = gain_flat[...].astype(jnp.float32).reshape(1, gain_flat.shape[0])

    def norm_part(p):
        def norm_rows(i, carry):
            at = pl.ds(pl.multiple_of(p * part + i * 16, 16), 16)
            floats = normed[at, :].astype(jnp.float32)
            inverse = lax.rsqrt(jnp.mean(floats * floats, axis=-1, keepdims=True) + 1e-05)
            normed[at, :] = (floats * inverse * gain_row[...]).astype(jnp.bfloat16)
            return carry

        lax.fori_loop(0, part // 16, norm_rows, 0)

    token_load(order(0)).wait()
    norm_part(order(0))

    @pl.when(middle)
    def _():
        pl.semaphore_wait(barrier, 4)

    @pl.when(jnp.logical_not(middle))
    def _():
        pl.semaphore_wait(barrier, 3)

    for s in range(SUBS):
        token_send(0, order(0), sub(s)).start()
    for i in range(2):
        for j in range(3):
            weight_copy(i, j, core).start()
    token_load(order(2)).wait()
    norm_part(order(2))
    for s in range(SUBS):
        token_send(2, order(2), sub(s)).start()
    for n in (1, 3, 4, 5):
        token_load(order(n)).wait()

    norm_part(order(1))
    lax.fori_loop(3, PARTS, lambda n, carry: (norm_part(order(n)), carry)[1], 0)

    def slab_start(slab):
        return (slabs[slab] * rows).astype(jnp.float32)

    def prepare():
        small_loads[1].wait()
        small_loads[2].wait()
        lane = lax.broadcasted_iota(jnp.int32, (1, HEAD_SIZE), 1)
        half = HEAD_SIZE // 2
        freqs = jnp.exp((lane % half).astype(jnp.float32) * (-2.0 * math.log(500000.0) / HEAD_SIZE))
        sign = jnp.where(lane < half, -1.0, 1.0)
        seg = segment_row[...]
        starts = [jnp.sum((seg < s).astype(jnp.float32)) for s in range(1, 4)]
        across = (lax.broadcasted_iota(jnp.int32, (1, lanes), 1) % part).astype(jnp.float32)

        def fill(p, carry):
            at = part_rows(p)
            first = (p * part).astype(jnp.float32)
            down = lax.broadcasted_iota(jnp.int32, (part, HEAD_SIZE), 0).astype(jnp.float32) + first
            for which, slab in ((0, t), (1, t_x)):
                angles = (down + slab_start(slab)) * freqs
                table[which, 0, at, :] = jnp.cos(angles)
                table[which, 1, at, :] = jnp.sin(angles) * sign
            place = across + first + slab_start(t)
            lowest = jnp.zeros_like(place)
            for start in starts:
                lowest = jnp.maximum(lowest, jnp.where(place >= start, start, 0.0))
            places[p] = place
            lows[p] = lowest
            return carry

        lax.fori_loop(0, PARTS, fill, 0)
        down = lax.broadcasted_iota(jnp.int32, (part, HEAD_SIZE), 0).astype(jnp.float32)
        for c in range(2):
            for x in range(2):
                first = (2 * c + x) * part
                kbase[first : first + part, :] = down + slab_start(2 * x + c)
        size = eye.shape[0]
        eye[...] = jnp.where(
            lax.broadcasted_iota(jnp.int32, (size, size), 0) == lax.broadcasted_iota(jnp.int32, (size, size), 1),
            1.0, 0.0,
        ).astype(jnp.bfloat16)

    def own_product(s):
        k = sub(s)
        columns = pl.ds(pl.multiple_of(x_index * near + k * depth, depth), depth)
        width = both

        def block(b, carry):
            at = pl.ds(pl.multiple_of(b * width, width), width)
            own[:, at] = own[:, at] + jnp.dot(
                normed[:, columns], wall[k, :, at], preferred_element_type=jnp.float32
            )
            return carry

        lax.fori_loop(0, own.shape[1] // width, block, 0)

    def relay(n, s):
        p = order(n)
        k = sub(s)
        inner_send(n, p, k).wait_recv()

        @pl.when(to_outer(n))
        def _():
            outer_send(n, p, k).start()

        @pl.when(to_inner(n))
        def _():
            inner_send(n, p, k).start()

    def send_own(n):
        skv[n, 1] = own[part_rows(order(n)), 0:both].astype(jnp.bfloat16)
        own_send(n).start()

    def emit(n, at):
        keep[n] = prem[at, 0:both]
        skv[n, 0] = prem[at, 0:both].astype(jnp.bfloat16)
        kv_send(n).start()
        sq[n] = prem[at, both:].astype(jnp.bfloat16)
        q_send(n).start()

    def turned(values, which, at):
        swapped = pltpu.roll(values, HEAD_SIZE // 2, 1)
        return (values * table[which, 0, at, :] + swapped * table[which, 1, at, :]).astype(jnp.bfloat16)

    def finish_keys(n):
        at = part_rows(order(n))

        def place(values, which, x):
            into = pl.ds(pl.multiple_of(core * 2 * part + x * part, part), part)
            for head in range(kv_heads):
                columns = slice(head * HEAD_SIZE, (head + 1) * HEAD_SIZE)
                kv[n, into, columns] = turned(values[:, columns], which, at)
            kv[n, into, kv_cols:both] = values[:, kv_cols:both].astype(jnp.bfloat16)

        own_send(n).wait_recv()
        kv_send(n).wait_recv()
        place(own[at, 0:both] + rkv[n, 0].astype(jnp.float32), 0, x_index)
        place(rkv[n, 1].astype(jnp.float32) + keep[n], 1, 1 - x_index)
        mate_copy(n, core).start()

    def finish_queries(n):
        at = part_rows(order(n))
        q_send(n).wait_recv()
        for head in range(heads):
            low = both + head * HEAD_SIZE
            values = own[at, low : low + HEAD_SIZE] + rq[
                n, :, head * HEAD_SIZE : (head + 1) * HEAD_SIZE
            ].astype(jnp.float32)
            first = (head % group_width) * part
            qrot[n, head // group_width, first : first + part, :] = turned(values, 0, at)

    factor = (HEAD_SIZE ** (-0.5)) * math.log2(math.e)
    pairs = (((1,), (1,)), ((), ()))

    def finish(n):
        finish_keys(n)
        finish_queries(n)

    def take(n):
        mate_copy(n, 1 - core).wait_recv()
        vt[n] = lax.dot_general(
            eye[...], kv[n, :, kv_cols:both], pairs, preferred_element_type=jnp.float32
        ).astype(jnp.bfloat16)

    def masked(i, j, where):
        offset = (order(j) * part).astype(jnp.float32)
        p = order(i)
        inside = (where <= places[p] - offset) & (where >= lows[p] - offset)
        bias = jnp.where(inside, 0.0, NEG)
        return [
            lax.dot_general(
                kv[j, :, h * HEAD_SIZE : (h + 1) * HEAD_SIZE], qrot[i, h], pairs,
                preferred_element_type=jnp.float32,
            ) + bias
            for h in range(kv_heads)
        ]

    def wide_base():
        return jnp.concatenate([kbase[...]] * (lanes // HEAD_SIZE), axis=1)

    def fresh(i, count):
        where = wide_base()
        blocks = [masked(i, j, where) for j in range(count)]
        for h in range(kv_heads):
            highest = blocks[0][h]
            for j in range(1, count):
                highest = jnp.maximum(highest, blocks[j][h])
            top = jnp.max(highest, axis=0, keepdims=True)
            exps = [jnp.exp2((blocks[j][h] - top) * factor) for j in range(count)]
            summed = exps[0]
            for j in range(1, count):
                summed = summed + exps[j]
            peak[i, h] = top
            total[i, h] = jnp.sum(summed, axis=0, keepdims=True)
            acc[i, h] = jnp.dot(
                jnp.concatenate([vt[j, h * HEAD_SIZE : (h + 1) * HEAD_SIZE, :] for j in range(count)], axis=1),
                jnp.concatenate([e.astype(jnp.bfloat16) for e in exps], axis=0),
                preferred_element_type=jnp.float32,
            )

    def earlier(j, count):
        where = wide_base()
        chains = [(i, h) for i in range(count) for h in range(kv_heads)]
        old = [peak[i, h] for i, h in chains]
        sums = [total[i, h] for i, h in chains]
        held = [acc[i, h] for i, h in chains]
        scores = [s for i in range(count) for s in masked(i, j, where)]
        new = [jnp.maximum(o, jnp.max(s, axis=0, keepdims=True)) for o, s in zip(old, scores)]
        exps = [jnp.exp2((s - top) * factor) for s, top in zip(scores, new)]
        mixed = [
            jnp.dot(
                vt[j, h * HEAD_SIZE : (h + 1) * HEAD_SIZE, :], e.astype(jnp.bfloat16),
                preferred_element_type=jnp.float32,
            )
            for (i, h), e in zip(chains, exps)
        ]
        for c, (i, h) in enumerate(chains):
            fade = jnp.exp2((old[c] - new[c]) * factor)
            peak[i, h] = new[c]
            total[i, h] = sums[c] * fade + jnp.sum(exps[c], axis=0, keepdims=True)
            acc[i, h] = held[c] * fade + mixed[c]

    prepare()
    own[...] = jnp.zeros_like(own)

    def first(s, carry):
        relay(0, s)
        for j in range(3):
            @pl.when(s < 2)
            def _():
                weight_load(s, j).wait()

            @pl.when(s >= 2)
            def _():
                weight_copy(s - 2, j, 1 - core).wait_recv()

        own_product(s)
        return carry

    lax.fori_loop(0, SUBS, first, 0)
    send_own(0)
    send_own(1)

    def pair(n, s, carry):
        k = sub(s)
        prem[...] = prem[...] + jnp.dot(
            jnp.concatenate([xrem[order(n), k], xrem[order(n + 1), k]], axis=0), wall[k],
            preferred_element_type=jnp.float32,
        )
        return carry

    prem[...] = jnp.zeros_like(prem)
    for s in range(3):
        relay(1, s)
    relay(2, 0)
    relay(1, 3)
    lax.fori_loop(0, 2, functools.partial(pair, 0), 0)
    relay(2, 1)
    lax.fori_loop(2, SUBS, functools.partial(pair, 0), 0)
    emit(0, slice(0, part))
    emit(1, slice(part, 2 * part))
    send_own(2)
    send_own(3)
    relay(2, 2)
    relay(2, 3)
    prem[...] = jnp.zeros_like(prem)

    def third(s, carry):
        relay(3, s)
        return pair(2, s, carry)

    lax.fori_loop(0, SUBS, third, 0)
    emit(2, slice(0, part))
    emit(3, slice(part, 2 * part))
    send_own(4)
    send_own(5)

    def single(u, carry):
        n = 4 + u // SUBS
        s = u % SUBS
        relay(n, s)
        k = sub(s)

        @pl.when(s == 0)
        def _():
            prem[0:part] = jnp.zeros((part, prem.shape[1]), jnp.float32)

        prem[0:part] = prem[0:part] + jnp.dot(xrem[order(n), k], wall[k], preferred_element_type=jnp.float32)

        @pl.when(s == SUBS - 1)
        def _():
            emit(n, slice(0, part))

        @pl.when(s < 2)
        def _():
            done = 2 * (u // SUBS) + s
            finish(done)
            take(done)

        @pl.when(u == SUBS)
        def _():
            lax.fori_loop(0, 3, lambda i, c: (fresh(i, 3), c)[1], 0)

        @pl.when(u == SUBS + 1)
        def _():
            earlier(3, 3)
            fresh(3, 4)

        return carry

    lax.fori_loop(0, 2 * SUBS, single, 0)
    finish(4)
    take(4)
    earlier(4, 4)
    fresh(4, 5)
    finish_keys(5)
    take(5)
    earlier(5, 5)

    def close(n, carry):
        at = part_rows(order(n))
        for h in range(kv_heads):
            scaled = (acc[n, h] * (1.0 / total[n, h])).astype(jnp.bfloat16)
            upright = lax.dot_general(eye[...], scaled, pairs, preferred_element_type=jnp.float32)
            for member in range(group_width):
                low = (h * group_width + member) * HEAD_SIZE
                out[at, low : low + HEAD_SIZE] = upright[member * part : (member + 1) * part].astype(jnp.bfloat16)
        return carry

    lax.fori_loop(0, PARTS - 1, close, 0)
    finish_queries(5)
    fresh(5, 6)
    close(5, 0)

    for i in range(2):
        for j in range(3):
            weight_copy(i, j, core).wait_send()

    def drain(n, carry):
        p = order(n)
        own_send(n).wait_send()
        kv_send(n).wait_send()
        q_send(n).wait_send()
        mate_copy(n, core).wait_send()
        for k in range(SUBS):
            @pl.when((n == 0) | (n == 2))
            def _():
                token_send(n, p, k).wait_send()

            @pl.when(to_inner(n))
            def _():
                inner_send(n, p, k).wait_send()

            @pl.when(to_outer(n))
            def _():
                outer_send(n, p, k).wait_send()

        return carry

    lax.fori_loop(0, PARTS, drain, 0)


def local_fused(tokens, norm_gain, w_query, w_key, value_weight, slab_order, segment_ids):
    rows, width = tokens.shape
    shard_rows, query_cols = w_query.shape
    kv_cols = w_key.shape[1]
    kv_heads = kv_cols // HEAD_SIZE
    group_width = query_cols // kv_cols
    columns = query_cols + 2 * kv_cols
    part = rows // PARTS
    depth = shard_rows // 2
    lanes = group_width * part
    hbm = pl.BlockSpec(memory_space=pl.ANY)
    half = jnp.bfloat16
    single = jnp.float32
    sem = pltpu.SemaphoreType.DMA
    return pl.pallas_call(
        fused_kernel,
        out_shape=pltpu.VMEM((rows, query_cols), jnp.bfloat16),
        in_specs=[hbm] * 7,
        out_specs=pl.BlockSpec(memory_space=pltpu.VMEM),
        scratch_shapes=[
            pltpu.VMEM((SUBS, depth, columns), half),
            pltpu.VMEM((rows, width), half),
            pltpu.VMEM((width,), half),
            pltpu.VMEM((1, width), single),
            pltpu.VMEM(segment_ids.shape, jnp.int32),
            pltpu.SMEM(slab_order.shape, jnp.int32),
            pltpu.VMEM((rows, columns), single),
            pltpu.VMEM((2 * part, columns), single),
            pltpu.VMEM((PARTS, SUBS, part, depth), half),
            pltpu.VMEM((PARTS, 2, part, 2 * kv_cols), half),
            pltpu.VMEM((PARTS, 2, part, 2 * kv_cols), half),
            pltpu.VMEM((PARTS, part, query_cols), half),
            pltpu.VMEM((PARTS, part, query_cols), half),
            pltpu.VMEM((PARTS, part, 2 * kv_cols), single),
            pltpu.VMEM((PARTS, kv_heads, lanes, HEAD_SIZE), half),
            pltpu.VMEM((PARTS, 4 * part, 2 * kv_cols), half),
            pltpu.VMEM((PARTS, kv_cols, 4 * part), half),
            pltpu.VMEM((2, 2, rows, HEAD_SIZE), single),
            pltpu.VMEM((PARTS, 1, lanes), single),
            pltpu.VMEM((PARTS, 1, lanes), single),
            pltpu.VMEM((4 * part, HEAD_SIZE), single),
            pltpu.VMEM((lanes, lanes), half),
            pltpu.VMEM((PARTS, kv_heads, 1, lanes), single),
            pltpu.VMEM((PARTS, kv_heads, 1, lanes), single),
            pltpu.VMEM((PARTS, kv_heads, HEAD_SIZE, lanes), single),
            sem((PARTS,)), sem((3,)), sem((2, 3)), sem((2, 3)), sem((2, 3)),
            sem((2, SUBS)), sem((PARTS, SUBS)), sem((PARTS, SUBS)), sem((PARTS, SUBS)),
            sem((PARTS, 2)), sem((PARTS, 2)), sem((PARTS,)), sem((PARTS,)), sem((PARTS,)), sem((PARTS,)),
        ],
        compiler_params=pltpu.CompilerParams(
            collective_id=0, has_side_effects=True, vmem_limit_bytes=58 << 20
        ),
        cost_estimate=pl.CostEstimate(
            flops=2 * rows * width * columns, bytes_accessed=40 << 20, transcendentals=rows * 4 * rows * 8
        ),
    )(tokens, norm_gain, w_query, w_key, value_weight, slab_order, segment_ids)


def solution(mesh):
    small = mesh.shape["ctx"] == 4 and mesh.shape["groups"] == 2 and mesh.shape["mp"] == 4
    local = local_fused if small else local_plain
    return jax.shard_map(
        local,
        mesh=mesh,
        in_specs=(
            P(("groups", "ctx"), None),
            P(),
            P("ctx", "mp"),
            P("ctx", "mp"),
            P("ctx", "mp"),
            P("groups"),
            P("groups"),
        ),
        out_specs=P(("groups", "ctx"), "mp"),
        check_vma=False,
    )
```

```python
import functools
import math

import jax
import jax.numpy as jnp
from jax import lax
from jax.experimental import pallas as pl
from jax.experimental.pallas import tpu as pltpu
from jax.sharding import PartitionSpec as P

HEAD_SIZE = 128


def apply_rotary(values, positions, heads):
    width = values.shape[1] // heads
    half = width // 2
    freqs = jnp.exp(jnp.arange(half, dtype=jnp.float32) * (-2.0 * math.log(500000.0) / width))
    angles = positions.astype(jnp.float32)[:, None] * freqs[None, :]
    cosine = jnp.cos(angles)[:, None, :]
    sine = jnp.sin(angles)[:, None, :]
    shaped = values.reshape(values.shape[0], heads, width)
    first = shaped[..., :half]
    second = shaped[..., half:]
    turned = jnp.concatenate(
        [first * cosine - second * sine, second * cosine + first * sine], axis=-1
    )
    return turned.reshape(values.shape)


def local_plain(tokens, norm_gain, w_query, w_key, value_weight, slab_order, segment_ids):
    tok_rows = tokens.shape[0]
    device_slab = lax.axis_index("ctx")
    position_all = (
        slab_order[:, None] * tok_rows + jnp.arange(tok_rows, dtype=jnp.int32)[None, :]
    ).reshape(-1)
    segment_all = jnp.take(segment_ids, position_all)
    my_position = lax.dynamic_slice_in_dim(position_all, device_slab * tok_rows, tok_rows)
    my_segment = lax.dynamic_slice_in_dim(segment_all, device_slab * tok_rows, tok_rows)
    floats = tokens.astype(jnp.float32)
    inverse = lax.rsqrt(jnp.mean(floats * floats, axis=-1, keepdims=True) + 1e-05)
    normed = (floats * inverse * norm_gain.astype(jnp.float32)[None, :]).astype(jnp.bfloat16)
    query_cols = w_query.shape[1]
    key_cols = w_key.shape[1]
    query = jnp.dot(
        normed,
        lax.all_gather(w_query, "ctx", axis=0, tiled=True),
        preferred_element_type=jnp.float32,
    )
    key_projected = jnp.dot(
        normed, lax.all_gather(w_key, "ctx", axis=0, tiled=True), preferred_element_type=jnp.float32
    )
    value_proj = jnp.dot(
        normed,
        lax.all_gather(value_weight, "ctx", axis=0, tiled=True),
        preferred_element_type=jnp.float32,
    )
    head_size = HEAD_SIZE
    heads_here = query_cols // head_size
    kv_here = key_cols // head_size
    group_width = heads_here // kv_here
    query_rot = (
        apply_rotary(query, my_position, heads_here)
        .astype(jnp.bfloat16)
        .reshape(tok_rows, kv_here, group_width, head_size)
    )
    key_rotary = apply_rotary(key_projected, my_position, kv_here).astype(jnp.bfloat16)
    value_b = value_proj.astype(jnp.bfloat16)
    scale = head_size ** (-0.5)
    start_state = (
        jnp.full((kv_here, group_width, tok_rows), -1e30, jnp.float32),
        jnp.zeros((kv_here, group_width, tok_rows), jnp.float32),
        jnp.zeros((kv_here, group_width, tok_rows, head_size), jnp.float32),
    )
    state = start_state
    key_piece = lax.all_gather(key_rotary, "ctx", axis=0, tiled=True)
    value_piece = lax.all_gather(value_b, "ctx", axis=0, tiled=True)
    piece_rows = key_piece.shape[0]
    block_rows = math.gcd(piece_rows, 1024)
    block_count = piece_rows // block_rows
    key_blocks = key_piece.reshape(block_count, block_rows, kv_here, head_size)
    value_blocks = value_piece.reshape(block_count, block_rows, kv_here, head_size)
    key_positions = position_all.reshape(block_count, block_rows)
    key_segments = segment_all.reshape(block_count, block_rows)

    def advance(inner, item):
        key_block, value_block, block_positions, block_segments = item
        allowed = (block_positions[None, :] <= my_position[:, None]) & (
            block_segments[None, :] == my_segment[:, None]
        )
        running_max, running_sum, running_acc = inner
        scores = (
            jnp.einsum("tkgd,nkd->kgtn", query_rot, key_block, preferred_element_type=jnp.float32)
            * scale
        )
        scores = jnp.where(allowed[None, None], scores, -1e30)
        new_max = jnp.maximum(running_max, jnp.max(scores, axis=-1))
        exps = jnp.where(allowed[None, None], jnp.exp(scores - new_max[..., None]), 0.0)
        factor = jnp.exp(running_max - new_max)
        new_sum = running_sum * factor + jnp.sum(exps, axis=-1)
        new_acc = running_acc * factor[..., None] + jnp.einsum(
            "kgtn,nkd->kgtd",
            exps.astype(jnp.bfloat16),
            value_block,
            preferred_element_type=jnp.float32,
        )
        inner = (new_max, new_sum, new_acc)
        return (inner, None)

    state, _ = lax.scan(advance, state, (key_blocks, value_blocks, key_positions, key_segments))
    final_max, final_sum, final_acc = state
    mixed = final_acc / final_sum[..., None]
    return (
        jnp.transpose(mixed, (2, 0, 1, 3))
        .reshape(tok_rows, heads_here * head_size)
        .astype(jnp.bfloat16)
    )


NEG = -1e30
PARTS = 6
SUBS = 4


def fused_kernel(
    tokens, gain, w_query, w_key, w_value, slab_order, segments, out,
    wall, normed, gain_flat, gain_row, segment_row, slabs, own, prem, xrem, skv, rkv, sq, rq, keep, qrot, kv, vt,
    table, places, lows, kbase, eye, peak, total, acc,
    tsem, ssem, wsem, ws, wr, xs, ins, outs, xr, kvs, kvr, qs, qr, cs, cr,
):
    g = lax.axis_index("groups")
    t = lax.axis_index("ctx")
    m = lax.axis_index("mp")
    x_index = t // 2
    core = t % 2
    t_core = x_index * 2 + (1 - core)
    t_x = (1 - x_index) * 2 + core
    middle = (m == 1) | (m == 2)
    core_dev = (g, t_core, m)
    x_dev = (g, t_x, m)
    inner_dev = (g, t, 1 + m % 2)
    outer_dev = (g, t, 3 * (m // 2))
    rows = tokens.shape[0]
    part = rows // PARTS
    depth = wall.shape[1]
    near = depth * SUBS
    kv_cols = w_key.shape[1]
    kv_heads = kv_cols // HEAD_SIZE
    both = 2 * kv_cols
    heads = w_query.shape[1] // HEAD_SIZE
    group_width = heads // kv_heads
    keys = 4 * part
    lanes = group_width * part

    def order(n):
        high = m // 2
        side = m + high * (3 - 2 * m)
        later = n // 3
        end = (2 * n) % 5 + 5 * (n // 5)
        mid = ((n % 3) * (1 + later) + 2 * (1 - later)) % 3 + 3 * later
        p = end * (1 - side) + mid * side
        return p + high * (5 - 2 * p)

    def part_rows(p):
        return pl.ds(pl.multiple_of(p * part, part), part)

    def remote(src, dst, send, recv, dev):
        return pltpu.make_async_remote_copy(
            src_ref=src, dst_ref=dst, send_sem=send, recv_sem=recv,
            device_id=dev, device_id_type=pl.DeviceIdType.MESH,
        )

    def sub(s):
        return (2 * core + s) % SUBS

    def token_load(p):
        return pltpu.make_async_copy(tokens.at[part_rows(p), :], normed.at[part_rows(p), :], tsem.at[p])

    sources = (
        (w_key, pl.ds(0, kv_cols)),
        (w_value, pl.ds(kv_cols, kv_cols)),
        (w_query, pl.ds(both, heads * HEAD_SIZE)),
    )

    def weight_load(i, j):
        source, columns = sources[j]
        return pltpu.make_async_copy(
            source.at[pl.ds(i * depth, depth), :], wall.at[2 * core + i, :, columns], wsem.at[i, j]
        )

    def weight_copy(i, j, c):
        source, columns = sources[j]
        return remote(
            source.at[pl.ds(i * depth, depth), :], wall.at[2 * c + i, :, columns],
            ws.at[i, j], wr.at[i, j], core_dev,
        )

    def token_send(n, p, k):
        columns = pl.ds(pl.multiple_of((1 - x_index) * near + k * depth, depth), depth)
        return remote(normed.at[part_rows(p), columns], xrem.at[p, k], xs.at[n // 2, k], xr.at[p, k], x_dev)

    def inner_send(n, p, k):
        return remote(xrem.at[p, k], xrem.at[p, k], ins.at[n, k], xr.at[p, k], inner_dev)

    def outer_send(n, p, k):
        return remote(xrem.at[p, k], xrem.at[p, k], outs.at[n, k], xr.at[p, k], outer_dev)

    def to_inner(n):
        return (n == 0) | (middle & (n <= 2))

    def to_outer(n):
        return middle & (n != 1) & (n != 5)

    def own_send(n):
        return remote(skv.at[n, 1], rkv.at[n, 1], kvs.at[n, 1], kvr.at[n, 1], x_dev)

    def kv_send(n):
        return remote(skv.at[n, 0], rkv.at[n, 0], kvs.at[n, 0], kvr.at[n, 0], x_dev)

    def q_send(n):
        return remote(sq.at[n], rq.at[n], qs.at[n], qr.at[n], x_dev)

    def mate_copy(n, c):
        view = kv.at[n, pl.ds(pl.multiple_of(c * 2 * part, 2 * part), 2 * part), :]
        return remote(view, view, cs.at[n], cr.at[n], core_dev)

    small_loads = (
        pltpu.make_async_copy(gain, gain_flat, ssem.at[0]),
        pltpu.make_async_copy(slab_order, slabs, ssem.at[1]),
        pltpu.make_async_copy(segments, segment_row, ssem.at[2]),
    )
    barrier = pltpu.get_barrier_semaphore()
    for dev in (x_dev, inner_dev, core_dev):
        pl.semaphore_signal(barrier, inc=1, device_id=dev, device_id_type=pl.DeviceIdType.MESH)

    @pl.when(middle)
    def _():
        pl.semaphore_signal(barrier, inc=1, device_id=outer_dev, device_id_type=pl.DeviceIdType.MESH)

    small_loads[0].start()
    for n in (0, 2, 1, 3, 4, 5):
        token_load(order(n)).start()
        if n == 0:
            small_loads[1].start()
            small_loads[2].start()
            for i in range(2):
                for j in range(3):
                    weight_load(i, j).start()
    small_loads[0].wait()
    gain_row[...] = gain_flat[...].astype(jnp.float32).reshape(1, gain_flat.shape[0])

    def norm_part(p):
        def norm_rows(i, carry):
            at = pl.ds(pl.multiple_of(p * part + i * 16, 16), 16)
            floats = normed[at, :].astype(jnp.float32)
            inverse = lax.rsqrt(jnp.mean(floats * floats, axis=-1, keepdims=True) + 1e-05)
            normed[at, :] = (floats * inverse * gain_row[...]).astype(jnp.bfloat16)
            return carry

        lax.fori_loop(0, part // 16, norm_rows, 0)

    token_load(order(0)).wait()
    norm_part(order(0))

    @pl.when(middle)
    def _():
        pl.semaphore_wait(barrier, 4)

    @pl.when(jnp.logical_not(middle))
    def _():
        pl.semaphore_wait(barrier, 3)

    for s in range(SUBS):
        token_send(0, order(0), sub(s)).start()
    for i in range(2):
        for j in range(3):
            weight_copy(i, j, core).start()
    token_load(order(2)).wait()
    norm_part(order(2))
    for s in range(SUBS):
        token_send(2, order(2), sub(s)).start()
    for n in (1, 3, 4, 5):
        token_load(order(n)).wait()

    norm_part(order(1))
    lax.fori_loop(3, PARTS, lambda n, carry: (norm_part(order(n)), carry)[1], 0)

    def slab_start(slab):
        return (slabs[slab] * rows).astype(jnp.float32)

    def prepare():
        small_loads[1].wait()
        small_loads[2].wait()
        lane = lax.broadcasted_iota(jnp.int32, (1, HEAD_SIZE), 1)
        half = HEAD_SIZE // 2
        freqs = jnp.exp((lane % half).astype(jnp.float32) * (-2.0 * math.log(500000.0) / HEAD_SIZE))
        sign = jnp.where(lane < half, -1.0, 1.0)
        seg = segment_row[...]
        starts = [jnp.sum((seg < s).astype(jnp.float32)) for s in range(1, 4)]
        across = (lax.broadcasted_iota(jnp.int32, (1, lanes), 1) % part).astype(jnp.float32)

        def fill(p, carry):
            at = part_rows(p)
            first = (p * part).astype(jnp.float32)
            down = lax.broadcasted_iota(jnp.int32, (part, HEAD_SIZE), 0).astype(jnp.float32) + first
            for which, slab in ((0, t), (1, t_x)):
                angles = (down + slab_start(slab)) * freqs
                table[which, 0, at, :] = jnp.cos(angles)
                table[which, 1, at, :] = jnp.sin(angles) * sign
            place = across + first + slab_start(t)
            lowest = jnp.zeros_like(place)
            for start in starts:
                lowest = jnp.maximum(lowest, jnp.where(place >= start, start, 0.0))
            places[p] = place
            lows[p] = lowest
            return carry

        lax.fori_loop(0, PARTS, fill, 0)
        down = lax.broadcasted_iota(jnp.int32, (part, HEAD_SIZE), 0).astype(jnp.float32)
        for c in range(2):
            for x in range(2):
                first = (2 * c + x) * part
                kbase[first : first + part, :] = down + slab_start(2 * x + c)
        size = eye.shape[0]
        eye[...] = jnp.where(
            lax.broadcasted_iota(jnp.int32, (size, size), 0) == lax.broadcasted_iota(jnp.int32, (size, size), 1),
            1.0, 0.0,
        ).astype(jnp.bfloat16)

    def own_product(s):
        k = sub(s)
        columns = pl.ds(pl.multiple_of(x_index * near + k * depth, depth), depth)
        width = both

        def block(b, carry):
            at = pl.ds(pl.multiple_of(b * width, width), width)
            own[:, at] = own[:, at] + jnp.dot(
                normed[:, columns], wall[k, :, at], preferred_element_type=jnp.float32
            )
            return carry

        lax.fori_loop(0, own.shape[1] // width, block, 0)

    def relay(n, s):
        p = order(n)
        k = sub(s)
        inner_send(n, p, k).wait_recv()

        @pl.when(to_outer(n))
        def _():
            outer_send(n, p, k).start()

        @pl.when(to_inner(n))
        def _():
            inner_send(n, p, k).start()

    def send_own(n):
        skv[n, 1] = own[part_rows(order(n)), 0:both].astype(jnp.bfloat16)
        own_send(n).start()

    def emit(n, at):
        keep[n] = prem[at, 0:both]
        skv[n, 0] = prem[at, 0:both].astype(jnp.bfloat16)
        kv_send(n).start()
        sq[n] = prem[at, both:].astype(jnp.bfloat16)
        q_send(n).start()

    def turned(values, which, at):
        swapped = pltpu.roll(values, HEAD_SIZE // 2, 1)
        return (values * table[which, 0, at, :] + swapped * table[which, 1, at, :]).astype(jnp.bfloat16)

    def finish_keys(n):
        at = part_rows(order(n))

        def place(values, which, x):
            into = pl.ds(pl.multiple_of(core * 2 * part + x * part, part), part)
            for head in range(kv_heads):
                columns = slice(head * HEAD_SIZE, (head + 1) * HEAD_SIZE)
                kv[n, into, columns] = turned(values[:, columns], which, at)
            kv[n, into, kv_cols:both] = values[:, kv_cols:both].astype(jnp.bfloat16)

        own_send(n).wait_recv()
        kv_send(n).wait_recv()
        place(own[at, 0:both] + rkv[n, 0].astype(jnp.float32), 0, x_index)
        place(rkv[n, 1].astype(jnp.float32) + keep[n], 1, 1 - x_index)
        mate_copy(n, core).start()

    def finish_queries(n):
        at = part_rows(order(n))
        q_send(n).wait_recv()
        for head in range(heads):
            low = both + head * HEAD_SIZE
            values = own[at, low : low + HEAD_SIZE] + rq[
                n, :, head * HEAD_SIZE : (head + 1) * HEAD_SIZE
            ].astype(jnp.float32)
            first = (head % group_width) * part
            qrot[n, head // group_width, first : first + part, :] = turned(values, 0, at)

    factor = (HEAD_SIZE ** (-0.5)) * math.log2(math.e)
    pairs = (((1,), (1,)), ((), ()))

    def finish(n):
        finish_keys(n)
        finish_queries(n)

    def take(n):
        mate_copy(n, 1 - core).wait_recv()
        vt[n] = lax.dot_general(
            eye[...], kv[n, :, kv_cols:both], pairs, preferred_element_type=jnp.float32
        ).astype(jnp.bfloat16)

    def masked(i, j, where):
        offset = (order(j) * part).astype(jnp.float32)
        p = order(i)
        inside = (where <= places[p] - offset) & (where >= lows[p] - offset)
        bias = jnp.where(inside, 0.0, NEG)
        return [
            lax.dot_general(
                kv[j, :, h * HEAD_SIZE : (h + 1) * HEAD_SIZE], qrot[i, h], pairs,
                preferred_element_type=jnp.float32,
            ) + bias
            for h in range(kv_heads)
        ]

    def wide_base():
        return jnp.concatenate([kbase[...]] * (lanes // HEAD_SIZE), axis=1)

    def fresh(i, count):
        where = wide_base()
        blocks = [masked(i, j, where) for j in range(count)]
        for h in range(kv_heads):
            highest = blocks[0][h]
            for j in range(1, count):
                highest = jnp.maximum(highest, blocks[j][h])
            top = jnp.max(highest, axis=0, keepdims=True)
            exps = [jnp.exp2((blocks[j][h] - top) * factor) for j in range(count)]
            summed = exps[0]
            for j in range(1, count):
                summed = summed + exps[j]
            peak[i, h] = top
            total[i, h] = jnp.sum(summed, axis=0, keepdims=True)
            acc[i, h] = jnp.dot(
                jnp.concatenate([vt[j, h * HEAD_SIZE : (h + 1) * HEAD_SIZE, :] for j in range(count)], axis=1),
                jnp.concatenate([e.astype(jnp.bfloat16) for e in exps], axis=0),
                preferred_element_type=jnp.float32,
            )

    def earlier(j, count):
        where = wide_base()
        chains = [(i, h) for i in range(count) for h in range(kv_heads)]
        old = [peak[i, h] for i, h in chains]
        sums = [total[i, h] for i, h in chains]
        held = [acc[i, h] for i, h in chains]
        scores = [s for i in range(count) for s in masked(i, j, where)]
        new = [jnp.maximum(o, jnp.max(s, axis=0, keepdims=True)) for o, s in zip(old, scores)]
        exps = [jnp.exp2((s - top) * factor) for s, top in zip(scores, new)]
        mixed = [
            jnp.dot(
                vt[j, h * HEAD_SIZE : (h + 1) * HEAD_SIZE, :], e.astype(jnp.bfloat16),
                preferred_element_type=jnp.float32,
            )
            for (i, h), e in zip(chains, exps)
        ]
        for c, (i, h) in enumerate(chains):
            fade = jnp.exp2((old[c] - new[c]) * factor)
            peak[i, h] = new[c]
            total[i, h] = sums[c] * fade + jnp.sum(exps[c], axis=0, keepdims=True)
            acc[i, h] = held[c] * fade + mixed[c]

    prepare()
    own[...] = jnp.zeros_like(own)

    def first(s, carry):
        relay(0, s)
        for j in range(3):
            @pl.when(s < 2)
            def _():
                weight_load(s, j).wait()

            @pl.when(s >= 2)
            def _():
                weight_copy(s - 2, j, 1 - core).wait_recv()

        own_product(s)
        return carry

    lax.fori_loop(0, SUBS, first, 0)
    send_own(0)
    send_own(1)

    def pair(n, s, carry):
        k = sub(s)
        prem[...] = prem[...] + jnp.dot(
            jnp.concatenate([xrem[order(n), k], xrem[order(n + 1), k]], axis=0), wall[k],
            preferred_element_type=jnp.float32,
        )
        return carry

    prem[...] = jnp.zeros_like(prem)
    for s in range(3):
        relay(1, s)
    relay(2, 0)
    relay(1, 3)
    lax.fori_loop(0, 2, functools.partial(pair, 0), 0)
    relay(2, 1)
    lax.fori_loop(2, SUBS, functools.partial(pair, 0), 0)
    emit(0, slice(0, part))
    emit(1, slice(part, 2 * part))
    send_own(2)
    send_own(3)
    relay(2, 2)
    relay(2, 3)
    prem[...] = jnp.zeros_like(prem)

    def third(s, carry):
        relay(3, s)
        return pair(2, s, carry)

    lax.fori_loop(0, SUBS, third, 0)
    emit(2, slice(0, part))
    emit(3, slice(part, 2 * part))
    send_own(4)
    send_own(5)

    def single(u, carry):
        n = 4 + u // SUBS
        s = u % SUBS
        relay(n, s)
        k = sub(s)

        @pl.when(s == 0)
        def _():
            prem[0:part] = jnp.zeros((part, prem.shape[1]), jnp.float32)

        prem[0:part] = prem[0:part] + jnp.dot(xrem[order(n), k], wall[k], preferred_element_type=jnp.float32)

        @pl.when(s == SUBS - 1)
        def _():
            emit(n, slice(0, part))

        @pl.when(s < 2)
        def _():
            done = 2 * (u // SUBS) + s
            finish(done)
            take(done)

        @pl.when((u == SUBS - 2) | (u == SUBS - 1))
        def _():
            fresh(u - SUBS + 2, 2)

        return carry

    lax.fori_loop(0, 2 * SUBS, single, 0)
    earlier(2, 2)
    fresh(2, 3)
    earlier(3, 3)
    fresh(3, 4)
    finish(4)
    take(4)
    earlier(4, 4)
    fresh(4, 5)
    finish_keys(5)
    take(5)
    earlier(5, 5)

    def close(n, carry):
        at = part_rows(order(n))
        for h in range(kv_heads):
            scaled = (acc[n, h] * (1.0 / total[n, h])).astype(jnp.bfloat16)
            upright = lax.dot_general(eye[...], scaled, pairs, preferred_element_type=jnp.float32)
            for member in range(group_width):
                low = (h * group_width + member) * HEAD_SIZE
                out[at, low : low + HEAD_SIZE] = upright[member * part : (member + 1) * part].astype(jnp.bfloat16)
        return carry

    lax.fori_loop(0, PARTS - 1, close, 0)
    finish_queries(5)
    fresh(5, 6)
    close(5, 0)

    for i in range(2):
        for j in range(3):
            weight_copy(i, j, core).wait_send()

    def drain(n, carry):
        p = order(n)
        own_send(n).wait_send()
        kv_send(n).wait_send()
        q_send(n).wait_send()
        mate_copy(n, core).wait_send()
        for k in range(SUBS):
            @pl.when((n == 0) | (n == 2))
            def _():
                token_send(n, p, k).wait_send()

            @pl.when(to_inner(n))
            def _():
                inner_send(n, p, k).wait_send()

            @pl.when(to_outer(n))
            def _():
                outer_send(n, p, k).wait_send()

        return carry

    lax.fori_loop(0, PARTS, drain, 0)


def local_fused(tokens, norm_gain, w_query, w_key, value_weight, slab_order, segment_ids):
    rows, width = tokens.shape
    shard_rows, query_cols = w_query.shape
    kv_cols = w_key.shape[1]
    kv_heads = kv_cols // HEAD_SIZE
    group_width = query_cols // kv_cols
    columns = query_cols + 2 * kv_cols
    part = rows // PARTS
    depth = shard_rows // 2
    lanes = group_width * part
    hbm = pl.BlockSpec(memory_space=pl.ANY)
    half = jnp.bfloat16
    single = jnp.float32
    sem = pltpu.SemaphoreType.DMA
    return pl.pallas_call(
        fused_kernel,
        out_shape=pltpu.VMEM((rows, query_cols), jnp.bfloat16),
        in_specs=[hbm] * 7,
        out_specs=pl.BlockSpec(memory_space=pltpu.VMEM),
        scratch_shapes=[
            pltpu.VMEM((SUBS, depth, columns), half),
            pltpu.VMEM((rows, width), half),
            pltpu.VMEM((width,), half),
            pltpu.VMEM((1, width), single),
            pltpu.VMEM(segment_ids.shape, jnp.int32),
            pltpu.SMEM(slab_order.shape, jnp.int32),
            pltpu.VMEM((rows, columns), single),
            pltpu.VMEM((2 * part, columns), single),
            pltpu.VMEM((PARTS, SUBS, part, depth), half),
            pltpu.VMEM((PARTS, 2, part, 2 * kv_cols), half),
            pltpu.VMEM((PARTS, 2, part, 2 * kv_cols), half),
            pltpu.VMEM((PARTS, part, query_cols), half),
            pltpu.VMEM((PARTS, part, query_cols), half),
            pltpu.VMEM((PARTS, part, 2 * kv_cols), single),
            pltpu.VMEM((PARTS, kv_heads, lanes, HEAD_SIZE), half),
            pltpu.VMEM((PARTS, 4 * part, 2 * kv_cols), half),
            pltpu.VMEM((PARTS, kv_cols, 4 * part), half),
            pltpu.VMEM((2, 2, rows, HEAD_SIZE), single),
            pltpu.VMEM((PARTS, 1, lanes), single),
            pltpu.VMEM((PARTS, 1, lanes), single),
            pltpu.VMEM((4 * part, HEAD_SIZE), single),
            pltpu.VMEM((lanes, lanes), half),
            pltpu.VMEM((PARTS, kv_heads, 1, lanes), single),
            pltpu.VMEM((PARTS, kv_heads, 1, lanes), single),
            pltpu.VMEM((PARTS, kv_heads, HEAD_SIZE, lanes), single),
            sem((PARTS,)), sem((3,)), sem((2, 3)), sem((2, 3)), sem((2, 3)),
            sem((2, SUBS)), sem((PARTS, SUBS)), sem((PARTS, SUBS)), sem((PARTS, SUBS)),
            sem((PARTS, 2)), sem((PARTS, 2)), sem((PARTS,)), sem((PARTS,)), sem((PARTS,)), sem((PARTS,)),
        ],
        compiler_params=pltpu.CompilerParams(
            collective_id=0, has_side_effects=True, vmem_limit_bytes=58 << 20
        ),
        cost_estimate=pl.CostEstimate(
            flops=2 * rows * width * columns, bytes_accessed=40 << 20, transcendentals=rows * 4 * rows * 8
        ),
    )(tokens, norm_gain, w_query, w_key, value_weight, slab_order, segment_ids)


def solution(mesh):
    small = mesh.shape["ctx"] == 4 and mesh.shape["groups"] == 2 and mesh.shape["mp"] == 4
    local = local_fused if small else local_plain
    return jax.shard_map(
        local,
        mesh=mesh,
        in_specs=(
            P(("groups", "ctx"), None),
            P(),
            P("ctx", "mp"),
            P("ctx", "mp"),
            P("ctx", "mp"),
            P("groups"),
            P("groups"),
        ),
        out_specs=P(("groups", "ctx"), "mp"),
        check_vma=False,
    )
```
